512 devices in a mesh: gather: 32 (over z, core), tm: 16 (over x, y).
Axes of the slice: x: 4, y: 4, z: 16, core: 2. Of those that a mesh axis runs over, the one named last changes fastest.
Arguments:
- records: bfloat16 [32, 4, 80, 2048], P('gather', None, None, 'tm'), may hold values from -6 to 6
- lift_weight: bfloat16 [32, 4], replicated, may hold values from -3 to 3
- lift_bias: float32 [32], replicated, may hold values from -2.5 to 2.5
- conv_weight: bfloat16 [4, 32, 32, 3, 3], replicated, may hold values from -0.375 to 0.375
- conv_bias: float32 [4, 32], replicated, may hold values from -1.5 to 1.5
- out_weight: bfloat16 [4, 32], replicated, may hold values from -1 to 1
- live_count: int32 [32], replicated, may hold values from 40 to 80, as said below
- trace_node: int32 [32, 80], replicated, may hold values from 0 to 79, as said below
- node_owner: int32 [80], replicated, may hold values from 0 to 31, as said below
Outputs:
- deblended: float32 [32, 4, 96, 2048], P(None, None, 'gather', 'tm')
The draws below stay inside these ranges and needn't reach their ends.
Inputs may be any that keep to these rules, and one draw needn't show every extreme that they name: `live_count`: some shot gather has all 80 traces live. `trace_node`: each row holds every node once; its first live_count slots hold consecutive nodes in rising order, and the others continue from there cyclically. `node_owner`: every index of gather owns 3 or 2 nodes, and some owns 3.
All inputs are finite; a program needn't handle non-finite values.
Results may differ from the reference program's by a relative error of at most 0.0039.
Values may be sent and summed in bfloat16 or wider, within the bound.
A program may use at most 64 MiB of HBM per device.

```python
import jax
import jax.numpy as jnp
from jax import lax

C = 32
COMPS = 4
NODES = 80
LAYERS = 2
HOLDERS = 32
SHOTS = 32
TIME = 2048
NODE_CAP = 3
NODE_SLOTS = 96


def shot_layout(key):
    base = jax.random.fold_in(key, 5)
    first_key, second_key, third_key = jax.random.split(base, 3)
    live = jax.random.randint(first_key, (SHOTS,), NODES // 2, NODES + 1)
    full_shot = jax.random.randint(second_key, (), 0, SHOTS)
    live = jnp.where(jnp.arange(SHOTS) == full_shot, NODES, live).astype(jnp.int32)
    start = jax.random.randint(third_key, (SHOTS,), 0, NODES - live + 1)
    nodes = (start[:, None] + jnp.arange(NODES)[None, :]) % NODES
    return (live, nodes.astype(jnp.int32))


def draw_live_count(key, part):
    return shot_layout(key)[0]


def draw_trace_node(key, part):
    return shot_layout(key)[1]


def draw_node_owner(key, part):
    order = jax.random.permutation(jax.random.fold_in(key, 9), NODES)
    return (order % HOLDERS).astype(jnp.int32)


def steps_of(key, shape, cuts, smallest, high):
    def one(dim, blocks):
        draws = jax.random.uniform(jax.random.fold_in(jax.random.fold_in(key, 6), dim), (blocks,), jnp.float32, smallest / len(cuts), high / len(cuts))
        return jnp.repeat(jnp.exp(draws), shape[dim] // blocks).reshape((-1,) + (1,) * (len(shape) - dim - 1))

    factor_of = one(*cuts[0])
    for cut in cuts[1:]:
        factor_of = factor_of * one(*cut)
    return factor_of


def bell_draw(rng, shape, width, bound, shards=(), kind=jnp.bfloat16):
    drawn = jax.random.normal(rng, shape, jnp.float32) * width
    if len(shards) > 0:
        drawn = steps_of(rng, shape, shards, -0.22, 0.18) * drawn
    return jnp.clip(drawn, min=-bound, max=bound).astype(kind)


def setup_inputs(seed: int = 0) -> dict:
    seeds = jax.random.split(jax.random.key(seed), 10)
    return {
        "records": bell_draw(seeds[0], (SHOTS, COMPS, NODES, TIME), 1.0, 6.0, ((0, 32), (3, 16))),
        "lift_weight": bell_draw(seeds[1], (C, COMPS), COMPS ** -0.5, 3.0),
        "lift_bias": bell_draw(seeds[2], (C,), 0.5, 2.5, (), jnp.float32),
        "conv_weight": bell_draw(seeds[3], (2 * LAYERS, C, C, 3, 3), (9 * C) ** -0.5, 0.375),
        "conv_bias": bell_draw(seeds[4], (2 * LAYERS, C), 0.3, 1.5, (), jnp.float32),
        "out_weight": bell_draw(seeds[5], (COMPS, C), C ** -0.5, 1.0),
        "live_count": draw_live_count(jax.random.fold_in(seeds[9], 71), 0),
        "trace_node": draw_trace_node(jax.random.fold_in(seeds[9], 71), 0),
        "node_owner": draw_node_owner(jax.random.fold_in(seeds[9], 71), 0),
    }


def dilated(field, kernel, dilation_factor):
    return lax.conv_general_dilated(field.astype(jnp.float32), kernel.astype(jnp.float32), (1, 1), ((dilation_factor, dilation_factor), (dilation_factor, dilation_factor)), rhs_dilation=(dilation_factor, dilation_factor), dimension_numbers=("NCHW", "OIHW", "NCHW"), precision=lax.Precision.HIGHEST, preferred_element_type=jnp.float32)


def residual_layer(field, kernel, bias_row, dilation_factor, keep_mask):
    summed = dilated(field, kernel, dilation_factor) + bias_row[None, :, None, None]
    return ((field.astype(jnp.float32) + jnp.maximum(summed, 0.0)) * keep_mask).astype(jnp.bfloat16)


def reference(records, lift_weight, lift_bias, conv_weight, conv_bias, out_weight, live_count, trace_node, node_owner):
    positions = jnp.arange(NODES, dtype=jnp.int32)
    same_owner = node_owner[:, None] == node_owner[None, :]
    earlier = positions[None, :] < positions[:, None]
    ranks = jnp.sum((same_owner & earlier).astype(jnp.int32), axis=1).astype(jnp.int32)
    slot_of_node = (node_owner * NODE_CAP + ranks).astype(jnp.int32)
    slot_table = slot_of_node[trace_node].astype(jnp.int32)
    live_table = positions[None, :] < live_count[:, None]
    lift_f = lift_weight.astype(jnp.float32)

    def shot_pass(inputs):
        record_block, live_row, slot_row = inputs
        keep_mask = live_row.astype(jnp.float32)[None, None, :, None]
        mixed = jnp.einsum("ck,kjt->cjt", lift_f, record_block.astype(jnp.float32), precision=lax.Precision.HIGHEST)
        hidden_state = ((mixed[None] + lift_bias[None, :, None, None]) * keep_mask).astype(jnp.bfloat16)
        for depth_level in range(LAYERS):
            hidden_state = residual_layer(hidden_state, conv_weight[depth_level], conv_bias[depth_level], 4 ** depth_level, keep_mask)
        placed = jnp.zeros((NODE_SLOTS, C, TIME), jnp.bfloat16).at[slot_row].set(jnp.transpose(hidden_state[0], (1, 0, 2)))
        live_records = record_block * live_row.astype(jnp.bfloat16)[None, :, None]
        placed_records = jnp.zeros((NODE_SLOTS, COMPS, TIME), jnp.bfloat16).at[slot_row].set(jnp.transpose(live_records, (1, 0, 2)))
        return placed, placed_records

    receiver_hidden, recv_records = lax.map(shot_pass, (records, live_table, slot_table))
    recv_live = jnp.zeros((SHOTS, NODE_SLOTS), jnp.float32).at[jnp.arange(SHOTS)[:, None], slot_table].set(live_table.astype(jnp.float32))
    out_f = out_weight.astype(jnp.float32)

    def node_pass(slot_index):
        gathered = lax.dynamic_index_in_dim(receiver_hidden, slot_index, axis=1, keepdims=False)
        rec_slot = lax.dynamic_index_in_dim(recv_records, slot_index, axis=1, keepdims=False)
        live_col = lax.dynamic_index_in_dim(recv_live, slot_index, axis=1, keepdims=False)
        keep_mask = live_col[None, None, :, None]
        hidden_state = jnp.transpose(gathered, (1, 0, 2))[None]
        for depth_level in range(LAYERS):
            hidden_state = residual_layer(hidden_state, conv_weight[LAYERS + depth_level], conv_bias[LAYERS + depth_level], 2 * 4 ** depth_level, keep_mask)
        noise = jnp.einsum("kc,cst->skt", out_f, hidden_state[0].astype(jnp.float32), precision=lax.Precision.HIGHEST)
        return (rec_slot.astype(jnp.float32) + noise) * live_col[:, None, None]

    per_slot = lax.map(node_pass, jnp.arange(NODE_SLOTS, dtype=jnp.int32))
    return jnp.transpose(per_slot, (1, 2, 0, 3))
```

```python
import functools

import jax
import jax.numpy as jnp
from jax import lax
from jax.experimental import pallas as pl
from jax.experimental.pallas import tpu as pltpu
from jax.sharding import PartitionSpec as P

F32 = jnp.float32
BF16 = jnp.bfloat16
MESH = pl.DeviceIdType.MESH
PIECES = 2
HALO = 16


def dot(left, right):
    return jnp.dot(left, right, preferred_element_type=F32)


def order_kernel(count_ref, trace_ref, records_ref, out_ref):
    me = lax.axis_index("gather")
    comps, nodes, span = records_ref.shape
    total = comps * nodes
    row = lax.broadcasted_iota(jnp.int32, (total, total), 0)
    trace = row // comps - trace_ref[me, 0]
    trace = jnp.where(trace < 0, trace + nodes, trace)
    wanted = jnp.where(trace < count_ref[me], (row % comps) * nodes + trace, -1)
    pick = (lax.broadcasted_iota(jnp.int32, (total, total), 1) == wanted).astype(F32).astype(BF16)
    out_ref[...] = dot(pick, records_ref[...].reshape(total, span)).astype(BF16)


def order(live_count, trace_node, records):
    comps, nodes, span = records.shape
    smem = pl.BlockSpec(memory_space=pltpu.SMEM)
    vmem = pl.BlockSpec(memory_space=pltpu.VMEM)
    rows = pl.pallas_call(
        order_kernel,
        out_shape=jax.ShapeDtypeStruct((nodes * comps, span), BF16),
        in_specs=[smem, smem, vmem],
        out_specs=vmem,
        name="order",
    )(live_count, trace_node, records)
    return rows.reshape(nodes, comps, span)


def one_hot(wanted, size):
    return (lax.broadcasted_iota(jnp.int32, (wanted.shape[0], size), 1) == wanted).astype(F32).astype(BF16)


def parts(value, count):
    found = []
    for _ in range(count):
        part = value.astype(BF16)
        found.append(part.astype(F32))
        value = value - found[-1]
    return found


def preparation(
    count_ref,
    trace_ref,
    owner_ref,
    lift_ref,
    lift_bias_ref,
    conv_ref,
    conv_bias_ref,
    project_ref,
    weight_ref,
    first_ref,
    out_weight_ref,
    bias_ref,
    keep_ref,
    live_ref,
    mask_ref,
    owned_ref,
    index_ref,
    spread_ref,
):
    nodes = owner_ref.shape[0]
    slots = owned_ref.shape[0]
    channels = conv_ref.shape[-1]

    def tile():
        row = lax.broadcasted_iota(jnp.int32, (channels, 256), 0)
        lane = lax.broadcasted_iota(jnp.int32, (channels, 256), 1)
        return (lane % channels == row).astype(F32).astype(BF16)

    def turned(left, right, left_dim, right_dim):
        return lax.dot_general(
            left, right, (((left_dim,), (right_dim,)), ((), ())), preferred_element_type=F32
        )

    def spread(layer):
        def step():
            for trace_tap in range(3):
                for time_tap in range(3):
                    spread_ref[(layer - 1) * 9 + trace_tap * 3 + time_tap] = turned(
                        conv_ref[layer, trace_tap, time_tap], tile(), 0, 0
                    ).astype(BF16)

        return step

    def banded(target, pairs):
        lane_group = lax.broadcasted_iota(jnp.int32, (32, 256), 1) // 32
        for place in range(8):
            total = jnp.zeros((32, 256), BF16)
            for shift, entry in pairs:
                if 0 <= place + shift < 8:
                    total = jnp.where(lane_group == place + shift, spread_ref[entry], total)
            weight_ref[target, pl.ds(place * 32, 32), :] = total

    def entry(layer, trace_tap, time_tap):
        return (layer - 1) * 9 + trace_tap * 3 + time_tap

    def second(trace_tap):
        def step():
            for time_tap in range(3):
                banded(trace_tap * 3 + time_tap, [(0, entry(1, trace_tap, time_tap))])

        return step

    def third():
        for time_tap in range(3):
            banded(9 + time_tap, [(0, entry(2, 1, time_tap))])
            banded(12 + time_tap, [(0, entry(2, 2, time_tap)), (1, entry(2, 0, time_tap))])
            banded(15 + time_tap, [(0, entry(2, 0, time_tap)), (-1, entry(2, 2, time_tap))])

    def fourth():
        for time_tap in range(3):
            banded(
                18 + time_tap,
                [(0, entry(3, 1, time_tap)), (2, entry(3, 0, time_tap)), (-2, entry(3, 2, time_tap))],
            )

    def lifted():
        bias = parts(lift_bias_ref[...], 3)
        zero = jnp.zeros((1, channels), F32)
        return jnp.concatenate([lift_ref[...].astype(F32)] + bias + [zero], axis=0)

    def row_marks(rows):
        row = lax.broadcasted_iota(jnp.int32, (rows, 1), 0)
        return row // 128, (row // 32) % 4, row % 4

    def block_mask(rows):
        row = lax.broadcasted_iota(jnp.int32, (rows, 256), 0)
        lane = lax.broadcasted_iota(jnp.int32, (rows, 256), 1)
        return (row // 4) % 8 == lane // 32

    def first_taps(time_tap):
        def step():
            part, offset, comp = row_marks(256)
            wanted = jnp.where(
                offset < 3, offset * 8 + comp, jnp.where(comp < 3, comp * 8 + 4, -1000)
            )
            pick = one_hot(wanted + part * 24, 48)
            rows = lifted().astype(BF16)
            folded = []
            for trace_tap in range(3):
                term = turned(rows, conv_ref[0, trace_tap, time_tap], 1, 1)
                number = lax.broadcasted_iota(jnp.int32, term.shape, 0)
                bias = term[4:5] + term[5:6] + term[6:7]
                folded.append(jnp.where(number == 4, bias, term))
            both = jnp.concatenate(parts(jnp.concatenate(folded, axis=0), 2), axis=0)
            chosen = dot(pick, both.astype(BF16)).astype(BF16)
            first_ref[time_tap] = jnp.where(block_mask(256), dot(chosen, tile()), 0.0).astype(BF16)

        return step

    def first_lift():
        part, offset, comp = row_marks(256)
        wanted = jnp.where((part == 0) & (offset == 1), comp, -1)
        wanted = jnp.where((part == 0) & (offset == 3) & (comp == 1), 4, wanted)
        wanted = jnp.where((part == 0) & (offset == 3) & (comp == 3), 5, wanted)
        wanted = jnp.where((part == 1) & (offset == 3) & (comp == 1), 6, wanted)
        chosen = dot(one_hot(wanted, 8), lifted().astype(BF16)).astype(BF16)
        first_ref[3] = jnp.where(block_mask(256), dot(chosen, tile()), 0.0).astype(BF16)

    def small():
        pick = one_hot(lax.broadcasted_iota(jnp.int32, (32, 1), 0) % 4, 8)
        project = jnp.concatenate(
            [project_ref[...].astype(F32), jnp.zeros((4, channels), F32)], axis=0
        )
        chosen = dot(pick, project.astype(BF16)).astype(BF16)
        out_weight_ref[...] = jnp.where(block_mask(32), dot(chosen, tile()), 0.0).astype(BF16)
        for layer in range(4):
            high, middle, low = parts(conv_bias_ref[pl.ds(layer, 1), :], 3)
            rows = jnp.concatenate([high, middle, low, jnp.zeros((5, channels), F32)], axis=0)
            wide = dot(rows.astype(BF16), tile())
            bias_ref[layer] = wide[0:1] + wide[1:2] + wide[2:3]

    def owned_nodes():
        me = lax.axis_index("gather")

        def look(node, carry):
            seen, found = carry[0], carry[1:]
            mine = owner_ref[node] == me
            found = tuple(
                jnp.where(mine & (seen == rank), node, value) for rank, value in enumerate(found)
            )
            return (seen + jnp.where(mine, 1, 0),) + found

        start = (jnp.int32(0),) + (jnp.int32(-1000),) * slots
        return lax.fori_loop(0, nodes, look, start)[1:]

    def places():
        found = owned_nodes()
        lane = lax.broadcasted_iota(jnp.int32, (1, 128), 1)
        for slot in range(slots):
            owned_ref[slot] = jnp.where(lane >= 0, jnp.where(found[slot] >= 0, 1.0, 0.0), 0.0)
            for trace_tap in range(3):
                group = slot * 3 + trace_tap
                middle = found[slot] + 4 * (trace_tap - 1)
                index_ref[27 + group] = middle
                around = middle - 1 + lane // 32
                inside = (around >= 0) & (around < nodes) & (lane < 96)
                keep_ref[group] = jnp.where(inside, 1.0, 0.0)
                for offset in range(3):
                    node = middle - 1 + offset
                    index_ref[group * 3 + offset] = jnp.clip(node, 0, nodes - 1)

    def liveness(tile_number):
        def step():
            wide = lax.broadcasted_iota(jnp.int32, (1, 256), 1)
            lane = lax.broadcasted_iota(jnp.int32, (1, 128), 1)

            def by_shot(place, read):
                total = jnp.zeros_like(place)
                for number in range(8):
                    total = jnp.where(place == number, read(tile_number + 4 * number), total)
                return total

            def start(shot):
                return trace_ref[shot, 0]

            def count(shot):
                return count_ref[shot]

            wide_start, wide_count = by_shot(wide // 32, start), by_shot(wide // 32, count)
            place = (lane % 32) // 4
            lane_start, lane_count = by_shot(place, start), by_shot(place, count)
            tap = jnp.where(lane % 4 < 3, lane % 4 - 1, 0)

            def alive(node, first_node, lives):
                trace = node - first_node
                trace = jnp.where(trace < 0, trace + nodes, trace)
                return (node >= 0) & (node < nodes) & (trace < lives)

            for group in range(slots * 3):
                middle = index_ref[27 + group]
                u = group * 4 + tile_number
                mask_ref[u] = jnp.where(alive(middle + 0 * wide, wide_start, wide_count), 1.0, 0.0)
                live_ref[u] = jnp.where(
                    alive(middle + tap, lane_start, lane_count) & (lane >= 96), 1.0, 0.0
                )

        return step

    return (
        [spread(1), places, first_taps(0), second(0), second(1), second(2), first_taps(1)]
        + [spread(2), first_taps(2), first_lift, third, small, spread(3), fourth]
        + [liveness(number) for number in range(4)]
    )


def share_kernel(holders, block_ref, *refs):
    sources, all_ref, results = refs[:8], refs[8], refs[9:18]
    spread_ref, local_sem, up_send, up_recv, down_send, down_recv, pair_send, pair_recv = refs[18:]
    work = preparation(*sources, *results, spread_ref)
    me = lax.axis_index("gather")
    chips = holders // 2
    chip, core = me // 2, lax.rem(me, 2)
    nodes = block_ref.shape[0]
    part = nodes // PIECES
    up = lax.rem(chip + 1, chips) * 2 + core
    down = lax.rem(chip + chips - 1, chips) * 2 + core
    pair = chip * 2 + 1 - core

    def place(position):
        shot = lax.rem(position + 2 * chips, chips) * 2 + core
        return lax.rem(shot, 4) * (holders // 4) + shot // 4

    def view(position, piece):
        return all_ref.at[pl.ds(piece * part, part), place(position)]

    def send(source, target, send_sem, recv_sem, device):
        copy = pltpu.make_async_remote_copy(
            src_ref=source,
            dst_ref=target,
            send_sem=send_sem,
            recv_sem=recv_sem,
            device_id={"gather": device},
            device_id_type=MESH,
        )
        copy.start()
        return copy

    barrier = pltpu.get_barrier_semaphore()
    for other in (up, down, pair):
        pl.semaphore_signal(barrier, inc=1, device_id={"gather": other}, device_id_type=MESH)
    local = pltpu.make_async_copy(block_ref, all_ref.at[:, place(chip)], local_sem)
    local.start()
    pl.semaphore_wait(barrier, 3)

    far = chips // 2
    started = []
    going_up, going_down = {}, {}
    for piece in range(PIECES):
        mine = block_ref.at[pl.ds(piece * part, part)]
        target = view(chip, piece)
        going_up[0, piece] = send(mine, target, up_send.at[0, piece], up_recv.at[0, piece], up)
        going_down[0, piece] = send(mine, target, down_send.at[0, piece], down_recv.at[0, piece], down)
    for piece in range(PIECES):
        mine = block_ref.at[pl.ds(piece * part, part)]
        started.append(send(mine, view(chip, piece), pair_send.at[0, piece], pair_recv.at[0, piece], pair))
    for step in range(1, far + 1):
        for number in range((step - 1) * len(work) // far, step * len(work) // far):
            work[number]()
        for piece in range(PIECES):
            if step < far or piece < PIECES // 2:
                going_up[step - 1, piece].wait_recv()
                held = view(chip - step, piece)
                if step + 1 < far or (step + 1 == far and piece < PIECES // 2):
                    going_up[step, piece] = send(held, held, up_send.at[step, piece], up_recv.at[step, piece], up)
                started.append(send(held, held, pair_send.at[step, piece], pair_recv.at[step, piece], pair))
            if step < far or piece >= PIECES // 2:
                going_down[step - 1, piece].wait_recv()
                held = view(chip + step, piece)
                if step + 1 < far or (step + 1 == far and piece >= PIECES // 2):
                    going_down[step, piece] = send(
                        held, held, down_send.at[step, piece], down_recv.at[step, piece], down
                    )
                slot = step if step == far else far + step
                started.append(send(held, held, pair_send.at[slot, piece], pair_recv.at[slot, piece], pair))
    for copy in list(going_up.values()) + list(going_down.values()):
        copy.wait_send()
    for copy in started:
        copy.wait()
    local.wait()


def share(holders, slots, blocks, sources):
    nodes, comps, window = blocks.shape
    far = holders // 4
    smem = pl.BlockSpec(memory_space=pltpu.SMEM)
    vmem = pl.BlockSpec(memory_space=pltpu.VMEM)
    anywhere = pl.BlockSpec(memory_space=pl.ANY)
    return pl.pallas_call(
        functools.partial(share_kernel, holders),
        out_shape=(
            jax.ShapeDtypeStruct((nodes, holders, comps, window), BF16),
            jax.ShapeDtypeStruct((21, 256, 256), BF16),
            jax.ShapeDtypeStruct((4, 256, 256), BF16),
            jax.ShapeDtypeStruct((32, 256), BF16),
            jax.ShapeDtypeStruct((4, 1, 256), F32),
            jax.ShapeDtypeStruct((slots * 3, 1, 128), F32),
            jax.ShapeDtypeStruct((slots * 12, 1, 128), F32),
            jax.ShapeDtypeStruct((slots * 12, 1, 256), F32),
            jax.ShapeDtypeStruct((slots, 1, 128), F32),
            jax.ShapeDtypeStruct((slots * 12,), jnp.int32),
        ),
        in_specs=[anywhere] + [smem] * 3 + [vmem] * 5,
        out_specs=(anywhere,) + (vmem,) * 8 + (smem,),
        scratch_shapes=[pltpu.VMEM((27, 32, 256), BF16), pltpu.SemaphoreType.DMA]
        + [pltpu.SemaphoreType.DMA((far, PIECES))] * 4
        + [pltpu.SemaphoreType.DMA((2 * far, PIECES))] * 2,
        compiler_params=pltpu.CompilerParams(
            collective_id=0, has_side_effects=True, vmem_limit_bytes=24 << 20
        ),
        name="share",
    )(blocks, *sources)


def layers_kernel(
    windows,
    index_ref,
    all_ref,
    keep_ref,
    live_ref,
    mask_ref,
    owned_ref,
    first_ref,
    weight,
    out_weight_ref,
    bias_ref,
    out_ref,
    field,
    first,
    second,
    third,
    send_sem,
    recv_sem,
):
    window_index = lax.axis_index("tm")
    right = lax.rem(window_index + 1, windows)
    left = lax.rem(window_index + windows - 1, windows)
    barrier = pltpu.get_barrier_semaphore()
    for other in (left, right):
        pl.semaphore_signal(barrier, inc=1, device_id={"tm": other}, device_id_type=MESH)

    slots = out_ref.shape[0]
    span = all_ref.shape[3]
    rows = span + 2 * HALO
    tiles = 4

    def turn(group, carry):
        near = [all_ref[index_ref[group * 3 + offset]] for offset in range(3)]
        for tile in range(tiles):
            stacked = jnp.concatenate([part[tile] for part in near] + [near[0][tile]], axis=0)
            turned = stacked.astype(F32).T
            u = group * tiles + tile
            field[u, pl.ds(HALO, span), :] = jnp.where(
                keep_ref[group] > 0.5, turned, live_ref[u]
            ).astype(BF16)
        return carry

    lax.fori_loop(0, slots * 3, turn, 0)

    pl.semaphore_wait(barrier, 2)
    copies = []
    for number, (source, target, device) in enumerate(((span, 0, right), (HALO, HALO + span, left))):
        copy = pltpu.make_async_remote_copy(
            src_ref=field.at[:, pl.ds(source, HALO), :],
            dst_ref=field.at[:, pl.ds(target, HALO), :],
            send_sem=send_sem.at[number],
            recv_sem=recv_sem.at[number],
            device_id={"tm": device},
            device_id_type=MESH,
        )
        copy.start()
        copies.append(copy)

    before = jnp.where(window_index > 0, 1.0, 0.0).astype(F32)
    after = jnp.where(window_index < windows - 1, 1.0, 0.0).astype(F32)

    def inside(value):
        return jnp.concatenate(
            [value[:HALO] * before, value[HALO : HALO + span], value[HALO + span :] * after], axis=0
        )

    for copy in copies:
        copy.wait()

    def ahead(value, by):
        return pltpu.roll(value, rows - by, 0)

    def behind(value, by):
        return pltpu.roll(value, by, 0)

    def first_layer(u, carry):
        here = jnp.concatenate(
            [
                (field[u, pl.ds(0, HALO), :].astype(F32) * before).astype(BF16),
                field[u, pl.ds(HALO, span), :],
                (field[u, pl.ds(HALO + span, HALO), :].astype(F32) * after).astype(BF16),
            ],
            axis=0,
        )
        here = jnp.concatenate([here, here], axis=1)
        total = dot(here, first_ref[1]) + behind(dot(here, first_ref[0]), 1) + ahead(dot(here, first_ref[2]), 1)
        grown = dot(here, first_ref[3]).astype(BF16).astype(F32) + jnp.maximum(total + bias_ref[0], 0.0)
        first[u] = inside(grown * mask_ref[u]).astype(BF16)
        return carry

    lax.fori_loop(0, slots * 3 * tiles, first_layer, 0, unroll=True)

    def second_layer(v, carry):
        slot, tile = v // tiles, lax.rem(v, tiles)
        sums = [None] * 3
        for trace_tap in range(3):
            u = (slot * 3 + trace_tap) * tiles + tile
            for time_tap in range(3):
                term = dot(first[u], weight[trace_tap * 3 + time_tap])
                sums[time_tap] = term if sums[time_tap] is None else sums[time_tap] + term
        total = sums[1] + behind(sums[0], 4) + ahead(sums[2], 4)
        center = (slot * 3 + 1) * tiles + tile
        grown = first[center].astype(F32) + jnp.maximum(total + bias_ref[1], 0.0)
        second[v] = inside(grown * mask_ref[center]).astype(BF16)
        return carry

    lax.fori_loop(0, slots * tiles, second_layer, 0, unroll=True)

    def third_layer(v, carry):
        slot, tile = v // tiles, lax.rem(v, tiles)
        half = tile // 2
        other = slot * tiles + lax.rem(tile + 2, tiles)
        sums = [
            dot(second[v], weight[9 + time_tap]) + dot(second[other], weight[12 + half * 3 + time_tap])
            for time_tap in range(3)
        ]
        total = sums[1] + behind(sums[0], 2) + ahead(sums[2], 2)
        center = (slot * 3 + 1) * tiles + tile
        grown = second[v].astype(F32) + jnp.maximum(total + bias_ref[2], 0.0)
        third[v] = inside(grown * mask_ref[center]).astype(BF16)
        return carry

    lax.fori_loop(0, slots * tiles, third_layer, 0, unroll=True)

    def fourth_layer(v, carry):
        slot, tile = v // tiles, lax.rem(v, tiles)
        early = dot(third[v, pl.ds(0, span + HALO), :], weight[18])[8 : 8 + span]
        middle = dot(third[v, pl.ds(HALO, span), :], weight[19])
        late = dot(third[v, pl.ds(HALO, span + HALO), :], weight[20])[8 : 8 + span]
        center = (slot * 3 + 1) * tiles + tile
        grown = third[v, pl.ds(HALO, span), :].astype(F32) + jnp.maximum(
            early + middle + late + bias_ref[3], 0.0
        )
        grown = (grown * mask_ref[center]).astype(BF16)
        noise = lax.dot_general(
            out_weight_ref[...], grown, (((1,), (1,)), ((), ())), preferred_element_type=F32
        )
        kept = all_ref[index_ref[slot * 9 + 4], tile].astype(F32)
        out_ref[slot, tile] = (kept + noise) * owned_ref[slot]
        return carry

    lax.fori_loop(0, slots * tiles, fourth_layer, 0, unroll=True)


def layers(windows, slots, index, shared, keep, live, mask, owned, first, weight, out_weight, bias):
    span = shared.shape[3]
    rows = span + 2 * HALO
    vmem = pl.BlockSpec(memory_space=pltpu.VMEM)
    return pl.pallas_call(
        functools.partial(layers_kernel, windows),
        out_shape=jax.ShapeDtypeStruct((slots, 4, 32, span), F32),
        in_specs=[pl.BlockSpec(memory_space=pltpu.SMEM)] + [vmem] * 9,
        out_specs=vmem,
        scratch_shapes=[
            pltpu.VMEM((slots * 12, rows, 128), BF16),
            pltpu.VMEM((slots * 12, rows, 256), BF16),
            pltpu.VMEM((slots * 4, rows, 256), BF16),
            pltpu.VMEM((slots * 4, rows, 256), BF16),
            pltpu.SemaphoreType.DMA((2,)),
            pltpu.SemaphoreType.DMA((2,)),
        ],
        compiler_params=pltpu.CompilerParams(
            collective_id=1, has_side_effects=True, vmem_limit_bytes=40 << 20
        ),
        name="layers",
    )(index, shared, keep, live, mask, owned, first, weight, out_weight, bias)


def body(
    records,
    lift_weight,
    lift_bias,
    conv_weight,
    conv_bias,
    out_weight,
    live_count,
    trace_node,
    node_owner,
):
    nodes, span = records.shape[2], records.shape[3]
    holders = lax.axis_size("gather")
    windows = lax.axis_size("tm")
    slots = (nodes + holders - 1) // holders
    sources = (
        live_count,
        trace_node,
        node_owner,
        lift_weight.T,
        lift_bias[None],
        jnp.transpose(conv_weight, (0, 3, 4, 1, 2)),
        conv_bias,
        out_weight,
    )
    shared, weight, first, project, bias, keep, live, mask, owned, index = share(
        holders, slots, order(live_count, trace_node, records[0]), sources
    )
    result = layers(
        windows,
        slots,
        index,
        shared.reshape(nodes, 4, 32, span),
        keep,
        live,
        mask,
        owned,
        first,
        weight,
        project,
        bias,
    )
    result = result.reshape(slots, 4, 8, 4, span)
    return jnp.transpose(result, (2, 1, 3, 0, 4)).reshape(32, 4, slots, span)


def solution(mesh):
    return jax.shard_map(
        body,
        mesh=mesh,
        in_specs=(P("gather", None, None, "tm"), P(), P(), P(), P(), P(), P(), P(), P()),
        out_specs=P(None, None, "gather", "tm"),
        check_vma=False,
    )
```

```python
import functools

import jax
import jax.numpy as jnp
from jax import lax
from jax.experimental import pallas as pl
from jax.experimental.pallas import tpu as pltpu
from jax.sharding import PartitionSpec as P

F32 = jnp.float32
BF16 = jnp.bfloat16
MESH = pl.DeviceIdType.MESH
PIECES = 2
HALO = 16


def dot(left, right):
    return jnp.dot(left, right, preferred_element_type=F32)


def order_kernel(count_ref, trace_ref, records_ref, out_ref):
    me = lax.axis_index("gather")
    comps, nodes, span = records_ref.shape
    total = comps * nodes
    row = lax.broadcasted_iota(jnp.int32, (total, total), 0)
    trace = row // comps - trace_ref[me, 0]
    trace = jnp.where(trace < 0, trace + nodes, trace)
    wanted = jnp.where(trace < count_ref[me], (row % comps) * nodes + trace, -1)
    pick = (lax.broadcasted_iota(jnp.int32, (total, total), 1) == wanted).astype(F32).astype(BF16)
    out_ref[...] = dot(pick, records_ref[...].reshape(total, span)).astype(BF16)


def order(live_count, trace_node, records):
    comps, nodes, span = records.shape
    smem = pl.BlockSpec(memory_space=pltpu.SMEM)
    vmem = pl.BlockSpec(memory_space=pltpu.VMEM)
    rows = pl.pallas_call(
        order_kernel,
        out_shape=jax.ShapeDtypeStruct((nodes * comps, span), BF16),
        in_specs=[smem, smem, vmem],
        out_specs=vmem,
        name="order",
    )(live_count, trace_node, records)
    return rows.reshape(nodes, comps, span)


def one_hot(wanted, size):
    return (lax.broadcasted_iota(jnp.int32, (wanted.shape[0], size), 1) == wanted).astype(F32).astype(BF16)


def parts(value, count):
    found = []
    for _ in range(count):
        part = value.astype(BF16)
        found.append(part.astype(F32))
        value = value - found[-1]
    return found


def preparation(
    count_ref,
    trace_ref,
    owner_ref,
    lift_ref,
    lift_bias_ref,
    conv_ref,
    conv_bias_ref,
    project_ref,
    weight_ref,
    first_ref,
    out_weight_ref,
    bias_ref,
    keep_ref,
    live_ref,
    mask_ref,
    owned_ref,
    index_ref,
    spread_ref,
):
    nodes = owner_ref.shape[0]
    slots = owned_ref.shape[0]
    channels = conv_ref.shape[-1]

    def tile():
        row = lax.broadcasted_iota(jnp.int32, (channels, 256), 0)
        lane = lax.broadcasted_iota(jnp.int32, (channels, 256), 1)
        return (lane % channels == row).astype(F32).astype(BF16)

    def turned(left, right, left_dim, right_dim):
        return lax.dot_general(
            left, right, (((left_dim,), (right_dim,)), ((), ())), preferred_element_type=F32
        )

    def spread(layer):
        def step():
            for trace_tap in range(3):
                for time_tap in range(3):
                    spread_ref[(layer - 1) * 9 + trace_tap * 3 + time_tap] = turned(
                        conv_ref[layer, trace_tap, time_tap], tile(), 0, 0
                    ).astype(BF16)

        return step

    def banded(target, pairs):
        lane_group = lax.broadcasted_iota(jnp.int32, (32, 256), 1) // 32
        for place in range(8):
            total = jnp.zeros((32, 256), BF16)
            for shift, entry in pairs:
                if 0 <= place + shift < 8:
                    total = jnp.where(lane_group == place + shift, spread_ref[entry], total)
            weight_ref[target, pl.ds(place * 32, 32), :] = total

    def entry(layer, trace_tap, time_tap):
        return (layer - 1) * 9 + trace_tap * 3 + time_tap

    def second(trace_tap):
        def step():
            for time_tap in range(3):
                banded(trace_tap * 3 + time_tap, [(0, entry(1, trace_tap, time_tap))])

        return step

    def third():
        for time_tap in range(3):
            banded(9 + time_tap, [(0, entry(2, 1, time_tap))])
            banded(12 + time_tap, [(0, entry(2, 2, time_tap)), (1, entry(2, 0, time_tap))])
            banded(15 + time_tap, [(0, entry(2, 0, time_tap)), (-1, entry(2, 2, time_tap))])

    def fourth():
        for time_tap in range(3):
            banded(
                18 + time_tap,
                [(0, entry(3, 1, time_tap)), (2, entry(3, 0, time_tap)), (-2, entry(3, 2, time_tap))],
            )

    def lifted():
        bias = parts(lift_bias_ref[...], 3)
        zero = jnp.zeros((1, channels), F32)
        return jnp.concatenate([lift_ref[...].astype(F32)] + bias + [zero], axis=0)

    def row_marks(rows):
        row = lax.broadcasted_iota(jnp.int32, (rows, 1), 0)
        return row // 128, (row // 32) % 4, row % 4

    def block_mask(rows):
        row = lax.broadcasted_iota(jnp.int32, (rows, 256), 0)
        lane = lax.broadcasted_iota(jnp.int32, (rows, 256), 1)
        return (row // 4) % 8 == lane // 32

    def first_taps(time_tap):
        def step():
            part, offset, comp = row_marks(256)
            wanted = jnp.where(
                offset < 3, offset * 8 + comp, jnp.where(comp < 3, comp * 8 + 4, -1000)
            )
            pick = one_hot(wanted + part * 24, 48)
            rows = lifted().astype(BF16)
            folded = []
            for trace_tap in range(3):
                term = turned(rows, conv_ref[0, trace_tap, time_tap], 1, 1)
                number = lax.broadcasted_iota(jnp.int32, term.shape, 0)
                bias = term[4:5] + term[5:6] + term[6:7]
                folded.append(jnp.where(number == 4, bias, term))
            both = jnp.concatenate(parts(jnp.concatenate(folded, axis=0), 2), axis=0)
            chosen = dot(pick, both.astype(BF16)).astype(BF16)
            first_ref[time_tap] = jnp.where(block_mask(256), dot(chosen, tile()), 0.0).astype(BF16)

        return step

    def first_lift():
        part, offset, comp = row_marks(256)
        wanted = jnp.where((part == 0) & (offset == 1), comp, -1)
        wanted = jnp.where((part == 0) & (offset == 3) & (comp == 1), 4, wanted)
        wanted = jnp.where((part == 0) & (offset == 3) & (comp == 3), 5, wanted)
        wanted = jnp.where((part == 1) & (offset == 3) & (comp == 1), 6, wanted)
        chosen = dot(one_hot(wanted, 8), lifted().astype(BF16)).astype(BF16)
        first_ref[3] = jnp.where(block_mask(256), dot(chosen, tile()), 0.0).astype(BF16)

    def small():
        pick = one_hot(lax.broadcasted_iota(jnp.int32, (32, 1), 0) % 4, 8)
        project = jnp.concatenate(
            [project_ref[...].astype(F32), jnp.zeros((4, channels), F32)], axis=0
        )
        chosen = dot(pick, project.astype(BF16)).astype(BF16)
        out_weight_ref[...] = jnp.where(block_mask(32), dot(chosen, tile()), 0.0).astype(BF16)
        for layer in range(4):
            high, middle, low = parts(conv_bias_ref[pl.ds(layer, 1), :], 3)
            rows = jnp.concatenate([high, middle, low, jnp.zeros((5, channels), F32)], axis=0)
            wide = dot(rows.astype(BF16), tile())
            bias_ref[layer] = wide[0:1] + wide[1:2] + wide[2:3]

    def owned_nodes():
        me = lax.axis_index("gather")

        def look(node, carry):
            seen, found = carry[0], carry[1:]
            mine = owner_ref[node] == me
            found = tuple(
                jnp.where(mine & (seen == rank), node, value) for rank, value in enumerate(found)
            )
            return (seen + jnp.where(mine, 1, 0),) + found

        start = (jnp.int32(0),) + (jnp.int32(-1000),) * slots
        return lax.fori_loop(0, nodes, look, start)[1:]

    def places():
        found = owned_nodes()
        lane = lax.broadcasted_iota(jnp.int32, (1, 128), 1)
        for slot in range(slots):
            owned_ref[slot] = jnp.where(lane >= 0, jnp.where(found[slot] >= 0, 1.0, 0.0), 0.0)
            for trace_tap in range(3):
                group = slot * 3 + trace_tap
                middle = found[slot] + 4 * (trace_tap - 1)
                index_ref[27 + group] = middle
                around = middle - 1 + lane // 32
                inside = (around >= 0) & (around < nodes) & (lane < 96)
                keep_ref[group] = jnp.where(inside, 1.0, 0.0)
                for offset in range(3):
                    node = middle - 1 + offset
                    index_ref[group * 3 + offset] = jnp.clip(node, 0, nodes - 1)

    def liveness(tile_number):
        def step():
            wide = lax.broadcasted_iota(jnp.int32, (1, 256), 1)
            lane = lax.broadcasted_iota(jnp.int32, (1, 128), 1)

            def by_shot(place, read):
                total = jnp.zeros_like(place)
                for number in range(8):
                    total = jnp.where(place == number, read(tile_number + 4 * number), total)
                return total

            def start(shot):
                return trace_ref[shot, 0]

            def count(shot):
                return count_ref[shot]

            wide_start, wide_count = by_shot(wide // 32, start), by_shot(wide // 32, count)
            place = (lane % 32) // 4
            lane_start, lane_count = by_shot(place, start), by_shot(place, count)
            tap = jnp.where(lane % 4 < 3, lane % 4 - 1, 0)

            def alive(node, first_node, lives):
                trace = node - first_node
                trace = jnp.where(trace < 0, trace + nodes, trace)
                return (node >= 0) & (node < nodes) & (trace < lives)

            for group in range(slots * 3):
                middle = index_ref[27 + group]
                u = group * 4 + tile_number
                mask_ref[u] = jnp.where(alive(middle + 0 * wide, wide_start, wide_count), 1.0, 0.0)
                live_ref[u] = jnp.where(
                    alive(middle + tap, lane_start, lane_count) & (lane >= 96), 1.0, 0.0
                )

        return step

    return (
        [spread(1), places, first_taps(0), second(0), second(1), second(2), first_taps(1)]
        + [spread(2), first_taps(2), first_lift, third, small, spread(3), fourth]
        + [liveness(number) for number in range(4)]
    )


HOPS = ((0, 2), (0, 1), (2, 4), (2, 3), (4, 6), (4, 5), (6, 8), (6, 7))


def share_kernel(holders, block_ref, *refs):
    sources, all_ref, results = refs[:8], refs[8], refs[9:18]
    spread_ref, local, built = refs[18], refs[19:27], refs[27:29]
    fetch_sem, local_sem, store_sem, send_sem, recv_sem, pair_send, pair_recv = refs[29:]
    fetches = []
    for number, (source, target) in enumerate(zip(sources, local)):
        fetches.append(pltpu.make_async_copy(source, target, fetch_sem.at[number]))
        fetches[-1].start()
    work = preparation(*local, *built, *results[2:], spread_ref)
    me = lax.axis_index("gather")
    chips = holders // 2
    far = chips // 2
    chip, core = me // 2, lax.rem(me, 2)
    nodes = block_ref.shape[0]
    part = nodes // PIECES
    pair = chip * 2 + 1 - core

    def at(offset):
        return lax.rem(chip + offset + 2 * chips, chips) * 2 + core

    def view(offset, piece):
        shot = at(offset)
        place = lax.rem(shot, 4) * (holders // 4) + shot // 4
        return all_ref.at[pl.ds(piece * part, part), place]

    def held(offset, piece):
        return block_ref.at[pl.ds(piece * part, part)] if offset == 0 else view(offset, piece)

    def send(offset, piece, send_sem, recv_sem, device):
        copy = pltpu.make_async_remote_copy(
            src_ref=held(offset, piece),
            dst_ref=view(offset, piece),
            send_sem=send_sem,
            recv_sem=recv_sem,
            device_id={"gather": device},
            device_id_type=MESH,
        )
        copy.start()
        return copy

    barrier = pltpu.get_barrier_semaphore()
    others = [pair] + [at(sign * hop) for hop in (1, 2) for sign in (1, -1)]
    for other in others:
        pl.semaphore_signal(barrier, inc=1, device_id={"gather": other}, device_id_type=MESH)
    mine = [
        pltpu.make_async_copy(held(0, piece), view(0, piece), local_sem.at[piece])
        for piece in range(PIECES)
    ]
    for copy in mine:
        copy.start()
    pl.semaphore_wait(barrier, len(others))

    def comes(sign, distance, piece):
        return distance < far or (piece < PIECES // 2) == (sign == 1)

    passed, handed = {}, []

    def forward(sign, distance, piece):
        side = 0 if sign == 1 else 1
        for start, stop in HOPS:
            if start == distance and comes(sign, stop, piece):
                passed[sign, stop, piece] = send(
                    -sign * distance,
                    piece,
                    send_sem.at[side, stop - 1, piece],
                    recv_sem.at[side, stop - 1, piece],
                    at(sign * (stop - start)),
                )

    def hand(sign, distance, piece):
        number = distance if sign == 1 or distance in (0, far) else far + distance
        handed.append(
            send(-sign * distance, piece, pair_send.at[number, piece], pair_recv.at[number, piece], pair)
        )

    for piece in range(PIECES):
        forward(1, 0, piece)
        forward(-1, 0, piece)
    for piece in range(PIECES):
        hand(1, 0, piece)
    for copy in fetches:
        copy.wait()
    for distance in range(1, far + 1):
        for number in range((distance - 1) * len(work) // far, distance * len(work) // far):
            work[number]()
        if distance == far:
            stores = [
                pltpu.make_async_copy(source, target, store_sem.at[number])
                for number, (source, target) in enumerate(zip(built, results[:2]))
            ]
            for copy in stores:
                copy.start()
        for piece in range(PIECES):
            for sign in (1, -1):
                if comes(sign, distance, piece):
                    passed[sign, distance, piece].wait_recv()
                    forward(sign, distance, piece)
                    hand(sign, distance, piece)
    for copy in passed.values():
        copy.wait_send()
    for copy in handed + mine + stores:
        copy.wait()


def share(holders, slots, blocks, sources):
    nodes, comps, window = blocks.shape
    far = holders // 4
    smem = pl.BlockSpec(memory_space=pltpu.SMEM)
    vmem = pl.BlockSpec(memory_space=pltpu.VMEM)
    local = [
        (pltpu.VMEM if number > 2 else pltpu.SMEM)(source.shape, source.dtype)
        for number, source in enumerate(sources)
    ]
    return pl.pallas_call(
        functools.partial(share_kernel, holders),
        out_shape=(
            jax.ShapeDtypeStruct((nodes, holders, comps, window), BF16),
            jax.ShapeDtypeStruct((21, 256, 256), BF16),
            jax.ShapeDtypeStruct((4, 256, 256), BF16),
            jax.ShapeDtypeStruct((32, 256), BF16),
            jax.ShapeDtypeStruct((4, 1, 256), F32),
            jax.ShapeDtypeStruct((slots * 3, 1, 128), F32),
            jax.ShapeDtypeStruct((slots * 12, 1, 128), F32),
            jax.ShapeDtypeStruct((slots * 12, 1, 256), F32),
            jax.ShapeDtypeStruct((slots, 1, 128), F32),
            jax.ShapeDtypeStruct((slots * 12,), jnp.int32),
        ),
        in_specs=[pl.BlockSpec(memory_space=pltpu.HBM)] * 9,
        out_specs=(pl.BlockSpec(memory_space=pltpu.HBM),) * 3 + (vmem,) * 6 + (smem,),
        scratch_shapes=[pltpu.VMEM((27, 32, 256), BF16)]
        + local
        + [pltpu.VMEM((21, 256, 256), BF16), pltpu.VMEM((4, 256, 256), BF16)]
        + [pltpu.SemaphoreType.DMA((8,)), pltpu.SemaphoreType.DMA((PIECES,)), pltpu.SemaphoreType.DMA((2,))]
        + [pltpu.SemaphoreType.DMA((2, far, PIECES))] * 2
        + [pltpu.SemaphoreType.DMA((2 * far, PIECES))] * 2,
        compiler_params=pltpu.CompilerParams(
            collective_id=0, has_side_effects=True, vmem_limit_bytes=60 << 20
        ),
        name="share",
    )(blocks, *sources)


def layers_kernel(
    windows,
    index_ref,
    all_source,
    keep_ref,
    live_ref,
    mask_ref,
    owned_ref,
    first_source,
    weight_source,
    out_weight_ref,
    bias_ref,
    out_ref,
    all_ref,
    first_ref,
    weight,
    field,
    first,
    second,
    third,
    fetch_sem,
    send_sem,
    recv_sem,
):
    window_index = lax.axis_index("tm")
    right = lax.rem(window_index + 1, windows)
    left = lax.rem(window_index + windows - 1, windows)
    barrier = pltpu.get_barrier_semaphore()
    for other in (left, right):
        pl.semaphore_signal(barrier, inc=1, device_id={"tm": other}, device_id_type=MESH)
    fetches = [
        pltpu.make_async_copy(source, target, fetch_sem.at[number])
        for number, (source, target) in enumerate(
            ((all_source, all_ref), (first_source, first_ref), (weight_source, weight))
        )
    ]
    for copy in fetches:
        copy.start()

    slots = out_ref.shape[0]
    span = all_ref.shape[3]
    tiles = 4

    def turn(group, carry):
        near = [all_ref[index_ref[group * 3 + offset]] for offset in range(3)]
        for tile in range(tiles):
            stacked = jnp.concatenate([part[tile] for part in near] + [near[0][tile]], axis=0)
            turned = stacked.astype(F32).T
            u = group * tiles + tile
            field[u, pl.ds(HALO, span), :] = jnp.where(
                keep_ref[group] > 0.5, turned, live_ref[u]
            ).astype(BF16)
        return carry

    fetches[0].wait()
    lax.fori_loop(0, slots * 3, turn, 0)

    pl.semaphore_wait(barrier, 2)
    copies = []
    for number, (source, target, device) in enumerate(((span, 0, right), (HALO, HALO + span, left))):
        copy = pltpu.make_async_remote_copy(
            src_ref=field.at[:, pl.ds(source, HALO), :],
            dst_ref=field.at[:, pl.ds(target, HALO), :],
            send_sem=send_sem.at[number],
            recv_sem=recv_sem.at[number],
            device_id={"tm": device},
            device_id_type=MESH,
        )
        copy.start()
        copies.append(copy)

    def ahead(value, by):
        return pltpu.roll(value, value.shape[0] - by, 0)

    def behind(value, by):
        return pltpu.roll(value, by, 0)

    def lift(here):
        here = jnp.concatenate([here, here], axis=1)
        total = dot(here, first_ref[1]) + behind(dot(here, first_ref[0]), 1) + ahead(dot(here, first_ref[2]), 1)
        return dot(here, first_ref[3]).astype(BF16).astype(F32) + jnp.maximum(total + bias_ref[0], 0.0)

    def inner(u, carry):
        first[u, pl.ds(HALO, span), :] = (lift(field[u, pl.ds(HALO, span), :]) * mask_ref[u]).astype(BF16)
        return carry

    fetches[1].wait()
    lax.fori_loop(0, slots * 3 * tiles, inner, 0, unroll=True)

    for copy in copies + fetches[2:]:
        copy.wait()

    before = jnp.where(window_index > 0, 1.0, 0.0).astype(F32)
    after = jnp.where(window_index < windows - 1, 1.0, 0.0).astype(F32)

    def inside(value):
        return jnp.concatenate(
            [value[:HALO] * before, value[HALO : HALO + span], value[HALO + span :] * after], axis=0
        )

    def edges(group, carry):
        pieces = []
        for tile in range(tiles):
            u = group * tiles + tile
            pieces.append((field[u, pl.ds(0, HALO), :].astype(F32) * before).astype(BF16))
            pieces.append(field[u, pl.ds(HALO, HALO), :])
            pieces.append(field[u, pl.ds(span, HALO), :])
            pieces.append((field[u, pl.ds(HALO + span, HALO), :].astype(F32) * after).astype(BF16))
        lifted = lift(jnp.concatenate(pieces, axis=0))
        for tile in range(tiles):
            u = group * tiles + tile
            here = lifted[tile * 4 * HALO : (tile + 1) * 4 * HALO] * mask_ref[u]
            low = first[u, pl.ds(HALO, HALO), :].astype(F32)
            high = first[u, pl.ds(span, HALO), :].astype(F32)
            first[u, pl.ds(0, 2 * HALO), :] = jnp.concatenate(
                [here[:HALO] * before, here[HALO : HALO + 8], low[8:]], axis=0
            ).astype(BF16)
            first[u, pl.ds(span, 2 * HALO), :] = jnp.concatenate(
                [high[:8], here[2 * HALO + 8 : 3 * HALO], here[3 * HALO :] * after], axis=0
            ).astype(BF16)
        return carry

    lax.fori_loop(0, slots * 3, edges, 0, unroll=True)

    def second_layer(v, carry):
        slot, tile = v // tiles, lax.rem(v, tiles)
        sums = [None] * 3
        for trace_tap in range(3):
            u = (slot * 3 + trace_tap) * tiles + tile
            for time_tap in range(3):
                term = dot(first[u], weight[trace_tap * 3 + time_tap])
                sums[time_tap] = term if sums[time_tap] is None else sums[time_tap] + term
        total = sums[1] + behind(sums[0], 4) + ahead(sums[2], 4)
        center = (slot * 3 + 1) * tiles + tile
        grown = first[center].astype(F32) + jnp.maximum(total + bias_ref[1], 0.0)
        second[v] = inside(grown * mask_ref[center]).astype(BF16)
        return carry

    lax.fori_loop(0, slots * tiles, second_layer, 0, unroll=True)

    def third_layer(v, carry):
        slot, tile = v // tiles, lax.rem(v, tiles)
        half = tile // 2
        other = slot * tiles + lax.rem(tile + 2, tiles)
        sums = [
            dot(second[v], weight[9 + time_tap]) + dot(second[other], weight[12 + half * 3 + time_tap])
            for time_tap in range(3)
        ]
        total = sums[1] + behind(sums[0], 2) + ahead(sums[2], 2)
        center = (slot * 3 + 1) * tiles + tile
        grown = second[v].astype(F32) + jnp.maximum(total + bias_ref[2], 0.0)
        third[v] = inside(grown * mask_ref[center]).astype(BF16)
        return carry

    lax.fori_loop(0, slots * tiles, third_layer, 0, unroll=True)

    def fourth_layer(v, carry):
        slot, tile = v // tiles, lax.rem(v, tiles)
        early = dot(third[v, pl.ds(0, span + HALO), :], weight[18])[8 : 8 + span]
        middle = dot(third[v, pl.ds(HALO, span), :], weight[19])
        late = dot(third[v, pl.ds(HALO, span + HALO), :], weight[20])[8 : 8 + span]
        center = (slot * 3 + 1) * tiles + tile
        grown = third[v, pl.ds(HALO, span), :].astype(F32) + jnp.maximum(
            early + middle + late + bias_ref[3], 0.0
        )
        grown = (grown * mask_ref[center]).astype(BF16)
        noise = lax.dot_general(
            out_weight_ref[...], grown, (((1,), (1,)), ((), ())), preferred_element_type=F32
        )
        kept = all_ref[index_ref[slot * 9 + 4], tile].astype(F32)
        out_ref[slot, tile] = (kept + noise) * owned_ref[slot]
        return carry

    lax.fori_loop(0, slots * tiles, fourth_layer, 0, unroll=True)


def layers(windows, slots, index, shared, keep, live, mask, owned, first, weight, out_weight, bias):
    span = shared.shape[3]
    rows = span + 2 * HALO
    vmem = pl.BlockSpec(memory_space=pltpu.VMEM)
    hbm = pl.BlockSpec(memory_space=pltpu.HBM)
    return pl.pallas_call(
        functools.partial(layers_kernel, windows),
        out_shape=jax.ShapeDtypeStruct((slots, 4, 32, span), F32),
        in_specs=[pl.BlockSpec(memory_space=pltpu.SMEM), hbm]
        + [vmem] * 4
        + [hbm, hbm]
        + [vmem] * 2,
        out_specs=vmem,
        scratch_shapes=[
            pltpu.VMEM(shared.shape, BF16),
            pltpu.VMEM(first.shape, BF16),
            pltpu.VMEM(weight.shape, BF16),
            pltpu.VMEM((slots * 12, rows, 128), BF16),
            pltpu.VMEM((slots * 12, rows, 256), BF16),
            pltpu.VMEM((slots * 4, rows, 256), BF16),
            pltpu.VMEM((slots * 4, rows, 256), BF16),
            pltpu.SemaphoreType.DMA((3,)),
            pltpu.SemaphoreType.DMA((2,)),
            pltpu.SemaphoreType.DMA((2,)),
        ],
        compiler_params=pltpu.CompilerParams(
            collective_id=1, has_side_effects=True, vmem_limit_bytes=60 << 20
        ),
        name="layers",
    )(index, shared, keep, live, mask, owned, first, weight, out_weight, bias)


def body(
    records,
    lift_weight,
    lift_bias,
    conv_weight,
    conv_bias,
    out_weight,
    live_count,
    trace_node,
    node_owner,
):
    nodes, span = records.shape[2], records.shape[3]
    holders = lax.axis_size("gather")
    windows = lax.axis_size("tm")
    slots = (nodes + holders - 1) // holders
    sources = (
        live_count,
        trace_node,
        node_owner,
        lift_weight.T,
        lift_bias[None],
        jnp.transpose(conv_weight, (0, 3, 4, 1, 2)),
        conv_bias,
        out_weight,
    )
    shared, weight, first, project, bias, keep, live, mask, owned, index = share(
        holders, slots, order(live_count, trace_node, records[0]), sources
    )
    result = layers(
        windows,
        slots,
        index,
        shared.reshape(nodes, 4, 32, span),
        keep,
        live,
        mask,
        owned,
        first,
        weight,
        project,
        bias,
    )
    result = result.reshape(slots, 4, 8, 4, span)
    return jnp.transpose(result, (2, 1, 3, 0, 4)).reshape(32, 4, slots, span)


def solution(mesh):
    return jax.shard_map(
        body,
        mesh=mesh,
        in_specs=(P("gather", None, None, "tm"), P(), P(), P(), P(), P(), P(), P(), P()),
        out_specs=P(None, None, "gather", "tm"),
        check_vma=False,
    )
```

```python
import functools

import jax
import jax.numpy as jnp
from jax import lax
from jax.experimental import pallas as pl
from jax.experimental.pallas import tpu as pltpu
from jax.sharding import PartitionSpec as P

F32 = jnp.float32
BF16 = jnp.bfloat16
MESH = pl.DeviceIdType.MESH
PIECES = 2
HALO = 16


def dot(left, right):
    return jnp.dot(left, right, preferred_element_type=F32)


def ordered(count_ref, trace_ref, records_ref):
    me = lax.axis_index("gather")
    comps, nodes, span = records_ref.shape
    total = comps * nodes
    row = lax.broadcasted_iota(jnp.int32, (total, total), 0)
    trace = row // comps - trace_ref[me, 0]
    trace = jnp.where(trace < 0, trace + nodes, trace)
    wanted = jnp.where(trace < count_ref[me], (row % comps) * nodes + trace, -1)
    pick = (lax.broadcasted_iota(jnp.int32, (total, total), 1) == wanted).astype(F32).astype(BF16)
    return dot(pick, records_ref[...].reshape(total, span)).astype(BF16).reshape(nodes, comps, span)


def one_hot(wanted, size):
    return (lax.broadcasted_iota(jnp.int32, (wanted.shape[0], size), 1) == wanted).astype(F32).astype(BF16)


def parts(value, count):
    found = []
    for _ in range(count):
        part = value.astype(BF16)
        found.append(part.astype(F32))
        value = value - found[-1]
    return found


def preparation(
    count_ref,
    trace_ref,
    owner_ref,
    lift_ref,
    lift_bias_ref,
    conv_ref,
    conv_bias_ref,
    project_ref,
    weight_ref,
    first_ref,
    out_weight_ref,
    bias_ref,
    keep_ref,
    live_ref,
    mask_ref,
    owned_ref,
    index_ref,
    spread_ref,
):
    nodes = owner_ref.shape[0]
    slots = owned_ref.shape[0]
    channels = conv_ref.shape[-1]

    def tile():
        row = lax.broadcasted_iota(jnp.int32, (channels, 256), 0)
        lane = lax.broadcasted_iota(jnp.int32, (channels, 256), 1)
        return (lane % channels == row).astype(F32).astype(BF16)

    def turned(left, right, left_dim, right_dim):
        return lax.dot_general(
            left, right, (((left_dim,), (right_dim,)), ((), ())), preferred_element_type=F32
        )

    def spread(layer):
        def step():
            for trace_tap in range(3):
                for time_tap in range(3):
                    spread_ref[(layer - 1) * 9 + trace_tap * 3 + time_tap] = turned(
                        conv_ref[layer, trace_tap, time_tap], tile(), 0, 0
                    ).astype(BF16)

        return step

    def banded(target, pairs):
        lane_group = lax.broadcasted_iota(jnp.int32, (32, 256), 1) // 32
        for place in range(8):
            total = jnp.zeros((32, 256), BF16)
            for shift, entry in pairs:
                if 0 <= place + shift < 8:
                    total = jnp.where(lane_group == place + shift, spread_ref[entry], total)
            weight_ref[target, pl.ds(place * 32, 32), :] = total

    def entry(layer, trace_tap, time_tap):
        return (layer - 1) * 9 + trace_tap * 3 + time_tap

    def second(trace_tap):
        def step():
            for time_tap in range(3):
                banded(trace_tap * 3 + time_tap, [(0, entry(1, trace_tap, time_tap))])

        return step

    def third():
        for time_tap in range(3):
            banded(9 + time_tap, [(0, entry(2, 1, time_tap))])
            banded(12 + time_tap, [(0, entry(2, 2, time_tap)), (1, entry(2, 0, time_tap))])
            banded(15 + time_tap, [(0, entry(2, 0, time_tap)), (-1, entry(2, 2, time_tap))])

    def fourth():
        for time_tap in range(3):
            banded(
                18 + time_tap,
                [(0, entry(3, 1, time_tap)), (2, entry(3, 0, time_tap)), (-2, entry(3, 2, time_tap))],
            )

    def lifted():
        bias = parts(lift_bias_ref[...], 3)
        zero = jnp.zeros((1, channels), F32)
        return jnp.concatenate([lift_ref[...].astype(F32)] + bias + [zero], axis=0)

    def row_marks(rows):
        row = lax.broadcasted_iota(jnp.int32, (rows, 1), 0)
        return row // 128, (row // 32) % 4, row % 4

    def block_mask(rows):
        row = lax.broadcasted_iota(jnp.int32, (rows, 256), 0)
        lane = lax.broadcasted_iota(jnp.int32, (rows, 256), 1)
        return (row // 4) % 8 == lane // 32

    def first_taps(time_tap):
        def step():
            part, offset, comp = row_marks(256)
            wanted = jnp.where(
                offset < 3, offset * 8 + comp, jnp.where(comp < 3, comp * 8 + 4, -1000)
            )
            pick = one_hot(wanted + part * 24, 48)
            rows = lifted().astype(BF16)
            folded = []
            for trace_tap in range(3):
                term = turned(rows, conv_ref[0, trace_tap, time_tap], 1, 1)
                number = lax.broadcasted_iota(jnp.int32, term.shape, 0)
                bias = term[4:5] + term[5:6] + term[6:7]
                folded.append(jnp.where(number == 4, bias, term))
            both = jnp.concatenate(parts(jnp.concatenate(folded, axis=0), 2), axis=0)
            chosen = dot(pick, both.astype(BF16)).astype(BF16)
            first_ref[time_tap] = jnp.where(block_mask(256), dot(chosen, tile()), 0.0).astype(BF16)

        return step

    def first_lift():
        part, offset, comp = row_marks(256)
        wanted = jnp.where((part == 0) & (offset == 1), comp, -1)
        wanted = jnp.where((part == 0) & (offset == 3) & (comp == 1), 4, wanted)
        wanted = jnp.where((part == 0) & (offset == 3) & (comp == 3), 5, wanted)
        wanted = jnp.where((part == 1) & (offset == 3) & (comp == 1), 6, wanted)
        chosen = dot(one_hot(wanted, 8), lifted().astype(BF16)).astype(BF16)
        first_ref[3] = jnp.where(block_mask(256), dot(chosen, tile()), 0.0).astype(BF16)

    def small():
        pick = one_hot(lax.broadcasted_iota(jnp.int32, (32, 1), 0) % 4, 8)
        project = jnp.concatenate(
            [project_ref[...].astype(F32), jnp.zeros((4, channels), F32)], axis=0
        )
        chosen = dot(pick, project.astype(BF16)).astype(BF16)
        out_weight_ref[...] = jnp.where(block_mask(32), dot(chosen, tile()), 0.0).astype(BF16)
        for layer in range(4):
            high, middle, low = parts(conv_bias_ref[pl.ds(layer, 1), :], 3)
            rows = jnp.concatenate([high, middle, low, jnp.zeros((5, channels), F32)], axis=0)
            wide = dot(rows.astype(BF16), tile())
            bias_ref[layer] = wide[0:1] + wide[1:2] + wide[2:3]

    def owned_nodes():
        me = lax.axis_index("gather")

        def look(node, carry):
            seen, found = carry[0], carry[1:]
            mine = owner_ref[node] == me
            found = tuple(
                jnp.where(mine & (seen == rank), node, value) for rank, value in enumerate(found)
            )
            return (seen + jnp.where(mine, 1, 0),) + found

        start = (jnp.int32(0),) + (jnp.int32(-1000),) * slots
        return lax.fori_loop(0, nodes, look, start)[1:]

    def places():
        found = owned_nodes()
        lane = lax.broadcasted_iota(jnp.int32, (1, 128), 1)
        for slot in range(slots):
            owned_ref[slot] = jnp.where(lane >= 0, jnp.where(found[slot] >= 0, 1.0, 0.0), 0.0)
            for trace_tap in range(3):
                group = slot * 3 + trace_tap
                middle = found[slot] + 4 * (trace_tap - 1)
                index_ref[27 + group] = middle
                around = middle - 1 + lane // 32
                inside = (around >= 0) & (around < nodes) & (lane < 96)
                keep_ref[group] = jnp.where(inside, 1.0, 0.0)
                for offset in range(3):
                    node = middle - 1 + offset
                    index_ref[group * 3 + offset] = jnp.clip(node, 0, nodes - 1)

    def liveness(tile_number):
        def step():
            wide = lax.broadcasted_iota(jnp.int32, (1, 256), 1)
            lane = lax.broadcasted_iota(jnp.int32, (1, 128), 1)

            def by_shot(place, read):
                total = jnp.zeros_like(place)
                for number in range(8):
                    total = jnp.where(place == number, read(tile_number + 4 * number), total)
                return total

            def start(shot):
                return trace_ref[shot, 0]

            def count(shot):
                return count_ref[shot]

            wide_start, wide_count = by_shot(wide // 32, start), by_shot(wide // 32, count)
            place = (lane % 32) // 4
            lane_start, lane_count = by_shot(place, start), by_shot(place, count)
            tap = jnp.where(lane % 4 < 3, lane % 4 - 1, 0)

            def alive(node, first_node, lives):
                trace = node - first_node
                trace = jnp.where(trace < 0, trace + nodes, trace)
                return (node >= 0) & (node < nodes) & (trace < lives)

            for group in range(slots * 3):
                middle = index_ref[27 + group]
                u = group * 4 + tile_number
                mask_ref[u] = jnp.where(alive(middle + 0 * wide, wide_start, wide_count), 1.0, 0.0)
                live_ref[u] = jnp.where(
                    alive(middle + tap, lane_start, lane_count) & (lane >= 96), 1.0, 0.0
                )

        return step

    return (
        [spread(1), places, first_taps(0), second(0), second(1), second(2), first_taps(1)]
        + [spread(2), first_taps(2), first_lift, third, small, spread(3), fourth]
        + [liveness(number) for number in range(4)]
    )


HOPS = ((0, 2), (0, 1), (2, 4), (2, 3), (4, 6), (4, 5), (6, 8), (6, 7))


def share(holders, windows, fetches, work, local, block_ref, all_ref, sems):
    local_sem, send_sem, recv_sem, pair_send, pair_recv = sems
    me = lax.axis_index("gather")
    chips = holders // 2
    far = chips // 2
    chip, core = me // 2, lax.rem(me, 2)
    nodes = block_ref.shape[0]
    part = nodes // PIECES
    pair = chip * 2 + 1 - core

    def at(offset):
        return lax.rem(chip + offset + 2 * chips, chips) * 2 + core

    def view(offset, piece):
        shot = at(offset)
        place = lax.rem(shot, 4) * (holders // 4) + shot // 4
        return all_ref.at[pl.ds(piece * part, part), place]

    def held(offset, piece):
        return block_ref.at[pl.ds(piece * part, part)] if offset == 0 else view(offset, piece)

    def send(offset, piece, send_sem, recv_sem, device):
        copy = pltpu.make_async_remote_copy(
            src_ref=held(offset, piece),
            dst_ref=view(offset, piece),
            send_sem=send_sem,
            recv_sem=recv_sem,
            device_id={"gather": device},
            device_id_type=MESH,
        )
        copy.start()
        return copy

    barrier = pltpu.get_barrier_semaphore()
    others = [pair] + [at(sign * hop) for hop in (1, 2) for sign in (1, -1)]
    for other in others:
        pl.semaphore_signal(barrier, inc=1, device_id={"gather": other}, device_id_type=MESH)
    window_index = lax.axis_index("tm")
    for step in (1, windows - 1):
        other = lax.rem(window_index + step, windows)
        pl.semaphore_signal(barrier, inc=1, device_id={"tm": other}, device_id_type=MESH)
    for copy in fetches[:3]:
        copy.wait()
    block_ref[...] = ordered(*local[:3])
    mine = [
        pltpu.make_async_copy(held(0, piece), view(0, piece), local_sem.at[piece])
        for piece in range(PIECES)
    ]
    for copy in mine:
        copy.start()
    pl.semaphore_wait(barrier, len(others) + 2)

    def comes(sign, distance, piece):
        return distance < far or (piece < PIECES // 2) == (sign == 1)

    passed, handed = {}, []

    def forward(sign, distance, piece):
        side = 0 if sign == 1 else 1
        for start, stop in HOPS:
            if start == distance and comes(sign, stop, piece):
                passed[sign, stop, piece] = send(
                    -sign * distance,
                    piece,
                    send_sem.at[side, stop - 1, piece],
                    recv_sem.at[side, stop - 1, piece],
                    at(sign * (stop - start)),
                )

    def hand(sign, distance, piece):
        number = distance if sign == 1 or distance in (0, far) else far + distance
        handed.append(
            send(-sign * distance, piece, pair_send.at[number, piece], pair_recv.at[number, piece], pair)
        )

    for piece in range(PIECES):
        forward(1, 0, piece)
        forward(-1, 0, piece)
    for piece in range(PIECES):
        hand(1, 0, piece)
    for copy in fetches[3:]:
        copy.wait()
    for distance in range(1, far + 1):
        for number in range((distance - 1) * len(work) // far, distance * len(work) // far):
            work[number]()
        for piece in range(PIECES):
            for sign in (1, -1):
                if comes(sign, distance, piece):
                    passed[sign, distance, piece].wait_recv()
                    forward(sign, distance, piece)
                    hand(sign, distance, piece)
    for copy in handed:
        copy.wait_recv()
    for copy in mine:
        copy.wait()
    return list(passed.values()) + handed


def compute(
    windows,
    all_ref,
    weight,
    first_ref,
    out_weight_ref,
    bias_ref,
    keep_ref,
    live_ref,
    mask_ref,
    owned_ref,
    index_ref,
    out_ref,
    field,
    first,
    second,
    third,
    send_sem,
    recv_sem,
):
    window_index = lax.axis_index("tm")
    right = lax.rem(window_index + 1, windows)
    left = lax.rem(window_index + windows - 1, windows)
    slots = owned_ref.shape[0]
    comps, span = all_ref.shape[2:]
    tiles = 4

    def turn(group, carry):
        near = [all_ref[index_ref[group * 3 + offset]].reshape(tiles, 32, span) for offset in range(3)]
        for tile in range(tiles):
            stacked = jnp.concatenate([part[tile] for part in near] + [near[0][tile]], axis=0)
            turned = stacked.astype(F32).T
            u = group * tiles + tile
            field[u, pl.ds(HALO, span), :] = jnp.where(
                keep_ref[group] > 0.5, turned, live_ref[u]
            ).astype(BF16)
        return carry

    lax.fori_loop(0, slots * 3, turn, 0)

    copies = []
    for number, (source, target, device) in enumerate(((span, 0, right), (HALO, HALO + span, left))):
        copy = pltpu.make_async_remote_copy(
            src_ref=field.at[:, pl.ds(source, HALO), :],
            dst_ref=field.at[:, pl.ds(target, HALO), :],
            send_sem=send_sem.at[number],
            recv_sem=recv_sem.at[number],
            device_id={"tm": device},
            device_id_type=MESH,
        )
        copy.start()
        copies.append(copy)

    def ahead(value, by):
        return pltpu.roll(value, value.shape[0] - by, 0)

    def behind(value, by):
        return pltpu.roll(value, by, 0)

    def lift(here):
        here = jnp.concatenate([here, here], axis=1)
        total = dot(here, first_ref[1]) + behind(dot(here, first_ref[0]), 1) + ahead(dot(here, first_ref[2]), 1)
        return dot(here, first_ref[3]).astype(BF16).astype(F32) + jnp.maximum(total + bias_ref[0], 0.0)

    def inner(u, carry):
        first[u, pl.ds(HALO, span), :] = (lift(field[u, pl.ds(HALO, span), :]) * mask_ref[u]).astype(BF16)
        return carry

    lax.fori_loop(0, slots * 3 * tiles, inner, 0, unroll=True)

    for copy in copies:
        copy.wait()

    before = jnp.where(window_index > 0, 1.0, 0.0).astype(F32)
    after = jnp.where(window_index < windows - 1, 1.0, 0.0).astype(F32)

    def inside(value):
        return jnp.concatenate(
            [value[:HALO] * before, value[HALO : HALO + span], value[HALO + span :] * after], axis=0
        )

    def edges(group, carry):
        pieces = []
        for tile in range(tiles):
            u = group * tiles + tile
            pieces.append((field[u, pl.ds(0, HALO), :].astype(F32) * before).astype(BF16))
            pieces.append(field[u, pl.ds(HALO, HALO), :])
            pieces.append(field[u, pl.ds(span, HALO), :])
            pieces.append((field[u, pl.ds(HALO + span, HALO), :].astype(F32) * after).astype(BF16))
        lifted = lift(jnp.concatenate(pieces, axis=0))
        for tile in range(tiles):
            u = group * tiles + tile
            here = lifted[tile * 4 * HALO : (tile + 1) * 4 * HALO] * mask_ref[u]
            low = first[u, pl.ds(HALO, HALO), :].astype(F32)
            high = first[u, pl.ds(span, HALO), :].astype(F32)
            first[u, pl.ds(0, 2 * HALO), :] = jnp.concatenate(
                [here[:HALO] * before, here[HALO : HALO + 8], low[8:]], axis=0
            ).astype(BF16)
            first[u, pl.ds(span, 2 * HALO), :] = jnp.concatenate(
                [high[:8], here[2 * HALO + 8 : 3 * HALO], here[3 * HALO :] * after], axis=0
            ).astype(BF16)
        return carry

    lax.fori_loop(0, slots * 3, edges, 0, unroll=True)

    def second_layer(v, carry):
        slot, tile = v // tiles, lax.rem(v, tiles)
        sums = [None] * 3
        for trace_tap in range(3):
            u = (slot * 3 + trace_tap) * tiles + tile
            for time_tap in range(3):
                term = dot(first[u], weight[trace_tap * 3 + time_tap])
                sums[time_tap] = term if sums[time_tap] is None else sums[time_tap] + term
        total = sums[1] + behind(sums[0], 4) + ahead(sums[2], 4)
        center = (slot * 3 + 1) * tiles + tile
        grown = first[center].astype(F32) + jnp.maximum(total + bias_ref[1], 0.0)
        second[v] = inside(grown * mask_ref[center]).astype(BF16)
        return carry

    lax.fori_loop(0, slots * tiles, second_layer, 0, unroll=True)

    def third_layer(v, carry):
        slot, tile = v // tiles, lax.rem(v, tiles)
        half = tile // 2
        other = slot * tiles + lax.rem(tile + 2, tiles)
        sums = [
            dot(second[v], weight[9 + time_tap]) + dot(second[other], weight[12 + half * 3 + time_tap])
            for time_tap in range(3)
        ]
        total = sums[1] + behind(sums[0], 2) + ahead(sums[2], 2)
        center = (slot * 3 + 1) * tiles + tile
        grown = second[v].astype(F32) + jnp.maximum(total + bias_ref[2], 0.0)
        third[v] = inside(grown * mask_ref[center]).astype(BF16)
        return carry

    lax.fori_loop(0, slots * tiles, third_layer, 0, unroll=True)

    def fourth_layer(v):
        slot, tile = v // tiles, v % tiles
        early = dot(third[v, pl.ds(0, span + HALO), :], weight[18])[8 : 8 + span]
        middle = dot(third[v, pl.ds(HALO, span), :], weight[19])
        late = dot(third[v, pl.ds(HALO, span + HALO), :], weight[20])[8 : 8 + span]
        center = (slot * 3 + 1) * tiles + tile
        grown = third[v, pl.ds(HALO, span), :].astype(F32) + jnp.maximum(
            early + middle + late + bias_ref[3], 0.0
        )
        grown = (grown * mask_ref[center]).astype(BF16)
        noise = lax.dot_general(
            out_weight_ref[...], grown, (((1,), (1,)), ((), ())), preferred_element_type=F32
        )
        kept = all_ref[index_ref[slot * 9 + 4]].reshape(tiles, 32, span)
        result = (kept[tile].astype(F32) + noise) * owned_ref[slot]
        out_ref[:, tile, slot] = result.reshape(8, comps, span)

    for v in range(slots * tiles):
        fourth_layer(v)


def whole_kernel(holders, windows, *refs):
    sources, out_ref = refs[:9], refs[9]
    local, tables, spread_ref = refs[10:19], refs[19:28], refs[28]
    block_ref, all_ref, layers = refs[29], refs[30], refs[31:35]
    fetch_sem, ring_sems, edge_sems = refs[35], refs[36:41], refs[41:43]
    fetches = []
    for number, (source, target) in enumerate(zip(sources, local)):
        fetches.append(pltpu.make_async_copy(source, target, fetch_sem.at[number]))
        fetches[-1].start()
    work = preparation(*local[:2], *local[3:], *tables, spread_ref)
    sends = share(holders, windows, fetches, work, local, block_ref, all_ref, ring_sems)
    compute(windows, all_ref, *tables, out_ref, *layers, *edge_sems)
    for copy in sends:
        copy.wait_send()


def table_shapes(slots):
    vmem = pltpu.VMEM
    return [
        vmem((21, 256, 256), BF16),
        vmem((4, 256, 256), BF16),
        vmem((32, 256), BF16),
        vmem((4, 1, 256), F32),
        vmem((slots * 3, 1, 128), F32),
        vmem((slots * 12, 1, 128), F32),
        vmem((slots * 12, 1, 256), F32),
        vmem((slots, 1, 128), F32),
        pltpu.SMEM((slots * 12,), jnp.int32),
    ]


def layer_shapes(slots, span):
    rows = span + 2 * HALO
    return [
        pltpu.VMEM((slots * 12, rows, 128), BF16),
        pltpu.VMEM((slots * 12, rows, 256), BF16),
        pltpu.VMEM((slots * 4, rows, 256), BF16),
        pltpu.VMEM((slots * 4, rows, 256), BF16),
    ]


def body(
    records,
    lift_weight,
    lift_bias,
    conv_weight,
    conv_bias,
    out_weight,
    live_count,
    trace_node,
    node_owner,
):
    comps, nodes, span = records.shape[1:]
    holders = lax.axis_size("gather")
    windows = lax.axis_size("tm")
    slots = (nodes + holders - 1) // holders
    far = holders // 4
    sources = (
        live_count,
        trace_node,
        records[0],
        node_owner,
        lift_weight.T,
        lift_bias[None],
        jnp.transpose(conv_weight, (0, 3, 4, 1, 2)),
        conv_bias,
        out_weight,
    )
    local = [
        (pltpu.SMEM if number in (0, 1, 3) else pltpu.VMEM)(source.shape, source.dtype)
        for number, source in enumerate(sources)
    ]
    dma = pltpu.SemaphoreType.DMA
    result = pl.pallas_call(
        functools.partial(whole_kernel, holders, windows),
        out_shape=jax.ShapeDtypeStruct((8, 4, slots, comps, span), F32),
        in_specs=[pl.BlockSpec(memory_space=pltpu.HBM)] * 9,
        out_specs=pl.BlockSpec(memory_space=pltpu.VMEM),
        scratch_shapes=local
        + table_shapes(slots)
        + [
            pltpu.VMEM((27, 32, 256), BF16),
            pltpu.VMEM((nodes, comps, span), BF16),
            pltpu.VMEM((nodes, holders, comps, span), BF16),
        ]
        + layer_shapes(slots, span)
        + [dma((9,)), dma((PIECES,))]
        + [dma((2, far, PIECES))] * 2
        + [dma((2 * far, PIECES))] * 2
        + [dma((2,)), dma((2,))],
        compiler_params=pltpu.CompilerParams(
            collective_id=0, has_side_effects=True, vmem_limit_bytes=60 << 20
        ),
        name="whole",
    )(*sources)
    return jnp.transpose(result, (0, 1, 3, 2, 4)).reshape(32, comps, slots, span)


def solution(mesh):
    return jax.shard_map(
        body,
        mesh=mesh,
        in_specs=(P("gather", None, None, "tm"), P(), P(), P(), P(), P(), P(), P(), P()),
        out_specs=P(None, None, "gather", "tm"),
        check_vma=False,
    )
```

```python
import functools

import jax
import jax.numpy as jnp
from jax import lax
from jax.experimental import pallas as pl
from jax.experimental.pallas import tpu as pltpu
from jax.sharding import PartitionSpec as P

F32 = jnp.float32
BF16 = jnp.bfloat16
MESH = pl.DeviceIdType.MESH
PIECES = 2
HALO = 16


def dot(left, right):
    return jnp.dot(left, right, preferred_element_type=F32)


def ordered(count_ref, trace_ref, records_ref):
    me = lax.axis_index("gather")
    comps, nodes, span = records_ref.shape
    total = comps * nodes
    row = lax.broadcasted_iota(jnp.int32, (total, total), 0)
    trace = row // comps - trace_ref[me, 0]
    trace = jnp.where(trace < 0, trace + nodes, trace)
    wanted = jnp.where(trace < count_ref[me], (row % comps) * nodes + trace, -1)
    pick = (lax.broadcasted_iota(jnp.int32, (total, total), 1) == wanted).astype(F32).astype(BF16)
    return dot(pick, records_ref[...].reshape(total, span)).astype(BF16).reshape(nodes, comps, span)


def one_hot(wanted, size):
    return (lax.broadcasted_iota(jnp.int32, (wanted.shape[0], size), 1) == wanted).astype(F32).astype(BF16)


def parts(value, count):
    found = []
    for _ in range(count):
        part = value.astype(BF16)
        found.append(part.astype(F32))
        value = value - found[-1]
    return found


def preparation(
    count_ref,
    trace_ref,
    owner_ref,
    lift_ref,
    lift_bias_ref,
    conv_ref,
    conv_bias_ref,
    project_ref,
    weight_ref,
    first_ref,
    out_weight_ref,
    bias_ref,
    keep_ref,
    live_ref,
    mask_ref,
    owned_ref,
    index_ref,
    spread_ref,
):
    nodes = owner_ref.shape[0]
    slots = owned_ref.shape[0]
    channels = conv_ref.shape[-1]

    def tile():
        row = lax.broadcasted_iota(jnp.int32, (channels, 256), 0)
        lane = lax.broadcasted_iota(jnp.int32, (channels, 256), 1)
        return (lane % channels == row).astype(F32).astype(BF16)

    def turned(left, right, left_dim, right_dim):
        return lax.dot_general(
            left, right, (((left_dim,), (right_dim,)), ((), ())), preferred_element_type=F32
        )

    def spread(layer):
        def step():
            for trace_tap in range(3):
                for time_tap in range(3):
                    spread_ref[layer * 9 + trace_tap * 3 + time_tap] = turned(
                        conv_ref[layer, trace_tap, time_tap], tile(), 0, 0
                    ).astype(BF16)

        return step

    def banded(target, pairs):
        lane_group = lax.broadcasted_iota(jnp.int32, (32, 256), 1) // 32
        for place in range(8):
            total = jnp.zeros((32, 256), BF16)
            for shift, entry in pairs:
                if 0 <= place + shift < 8:
                    total = jnp.where(lane_group == place + shift, spread_ref[entry], total)
            weight_ref[target, pl.ds(place * 32, 32), :] = total

    def entry(layer, trace_tap, time_tap):
        return layer * 9 + trace_tap * 3 + time_tap

    def plain(target, layer, trace_tap):
        def step():
            for time_tap in range(3):
                banded(target + trace_tap * 3 + time_tap, [(0, entry(layer, trace_tap, time_tap))])

        return step

    def third():
        for time_tap in range(3):
            banded(9 + time_tap, [(0, entry(2, 1, time_tap))])
            banded(12 + time_tap, [(0, entry(2, 2, time_tap)), (1, entry(2, 0, time_tap))])
            banded(15 + time_tap, [(0, entry(2, 0, time_tap)), (-1, entry(2, 2, time_tap))])

    def fourth():
        for time_tap in range(3):
            banded(
                18 + time_tap,
                [(0, entry(3, 1, time_tap)), (2, entry(3, 0, time_tap)), (-2, entry(3, 2, time_tap))],
            )

    def lifted():
        bias = parts(lift_bias_ref[...], 3)
        zero = jnp.zeros((1, channels), F32)
        return jnp.concatenate([lift_ref[...].astype(F32)] + bias + [zero], axis=0)

    def row_marks(rows):
        row = lax.broadcasted_iota(jnp.int32, (rows, 1), 0)
        return row // 128, (row // 32) % 4, row % 4

    def block_mask(rows):
        row = lax.broadcasted_iota(jnp.int32, (rows, 256), 0)
        lane = lax.broadcasted_iota(jnp.int32, (rows, 256), 1)
        return (row // 4) % 8 == lane // 32

    def lifts():
        part, offset, comp = row_marks(256)
        rows = lifted().astype(BF16)
        for trace_tap in range(3):
            alive = (offset == 3) & (comp == trace_tap)
            wanted = jnp.where((part == 0) & (offset == trace_tap), comp, -1)
            wanted = jnp.where(alive & (part == 0), 4, jnp.where(alive & (part == 1), 5, wanted))
            chosen = dot(one_hot(wanted, 8), rows).astype(BF16)
            first_ref[trace_tap] = jnp.where(block_mask(256), dot(chosen, tile()), 0.0).astype(BF16)

    def small():
        pick = one_hot(lax.broadcasted_iota(jnp.int32, (32, 1), 0) % 4, 8)
        project = jnp.concatenate(
            [project_ref[...].astype(F32), jnp.zeros((4, channels), F32)], axis=0
        )
        chosen = dot(pick, project.astype(BF16)).astype(BF16)
        out_weight_ref[...] = jnp.where(block_mask(32), dot(chosen, tile()), 0.0).astype(BF16)
        for layer in range(4):
            high, middle, low = parts(conv_bias_ref[pl.ds(layer, 1), :], 3)
            rows = jnp.concatenate([high, middle, low, jnp.zeros((5, channels), F32)], axis=0)
            wide = dot(rows.astype(BF16), tile())
            bias_ref[layer] = wide[0:1] + wide[1:2] + wide[2:3]

    def owned_nodes():
        me = lax.axis_index("gather")

        def look(node, carry):
            seen, found = carry[0], carry[1:]
            mine = owner_ref[node] == me
            found = tuple(
                jnp.where(mine & (seen == rank), node, value) for rank, value in enumerate(found)
            )
            return (seen + jnp.where(mine, 1, 0),) + found

        start = (jnp.int32(0),) + (jnp.int32(-1000),) * slots
        return lax.fori_loop(0, nodes, look, start)[1:]

    def places():
        found = owned_nodes()
        lane = lax.broadcasted_iota(jnp.int32, (1, 128), 1)
        for slot in range(slots):
            owned_ref[slot] = jnp.where(lane >= 0, jnp.where(found[slot] >= 0, 1.0, 0.0), 0.0)
            for trace_tap in range(3):
                group = slot * 3 + trace_tap
                middle = found[slot] + 4 * (trace_tap - 1)
                index_ref[27 + group] = middle
                around = middle - 1 + lane // 32
                inside = (around >= 0) & (around < nodes) & (lane < 96)
                keep_ref[group] = jnp.where(inside, 1.0, 0.0)
                for offset in range(3):
                    node = middle - 1 + offset
                    index_ref[group * 3 + offset] = jnp.clip(node, 0, nodes - 1)

    def liveness(tile_number):
        def step():
            wide = lax.broadcasted_iota(jnp.int32, (1, 256), 1)
            lane = lax.broadcasted_iota(jnp.int32, (1, 128), 1)

            def by_shot(place, read):
                total = jnp.zeros_like(place)
                for number in range(8):
                    total = jnp.where(place == number, read(tile_number + 4 * number), total)
                return total

            def start(shot):
                return trace_ref[shot, 0]

            def count(shot):
                return count_ref[shot]

            wide_start, wide_count = by_shot(wide // 32, start), by_shot(wide // 32, count)
            place = (lane % 32) // 4
            lane_start, lane_count = by_shot(place, start), by_shot(place, count)
            tap = jnp.where(lane % 4 < 3, lane % 4 - 1, 0)

            def alive(node, first_node, lives):
                trace = node - first_node
                trace = jnp.where(trace < 0, trace + nodes, trace)
                return (node >= 0) & (node < nodes) & (trace < lives)

            for group in range(slots * 3):
                middle = index_ref[27 + group]
                u = group * 4 + tile_number
                mask_ref[u] = jnp.where(alive(middle + 0 * wide, wide_start, wide_count), 1.0, 0.0)
                live_ref[u] = jnp.where(
                    alive(middle + tap, lane_start, lane_count) & (lane >= 96), 1.0, 0.0
                )

        return step

    return (
        [spread(0), places, lifts, plain(21, 0, 0), plain(21, 0, 1), plain(21, 0, 2), spread(1)]
        + [plain(0, 1, 0), plain(0, 1, 1), plain(0, 1, 2), spread(2), third, small, spread(3), fourth]
        + [liveness(number) for number in range(4)]
    )


HOPS = ((0, 1), (1, 3), (1, 2), (3, 5), (3, 4), (5, 7), (5, 6), (7, 8))


def share(holders, windows, fetches, work, local, block_ref, all_ref, sems):
    local_sem, send_sem, recv_sem, pair_send, pair_recv = sems
    me = lax.axis_index("gather")
    chips = holders // 2
    far = chips // 2
    chip, core = me // 2, lax.rem(me, 2)
    nodes = block_ref.shape[0]
    part = nodes // PIECES
    pair = chip * 2 + 1 - core

    def at(offset):
        return lax.rem(chip + offset + 2 * chips, chips) * 2 + core

    def view(offset, piece):
        shot = at(offset)
        place = lax.rem(shot, 4) * (holders // 4) + shot // 4
        return all_ref.at[pl.ds(piece * part, part), place]

    def held(offset, piece):
        return block_ref.at[pl.ds(piece * part, part)] if offset == 0 else view(offset, piece)

    def send(offset, piece, send_sem, recv_sem, device):
        copy = pltpu.make_async_remote_copy(
            src_ref=held(offset, piece),
            dst_ref=view(offset, piece),
            send_sem=send_sem,
            recv_sem=recv_sem,
            device_id={"gather": device},
            device_id_type=MESH,
        )
        copy.start()
        return copy

    barrier = pltpu.get_barrier_semaphore()
    others = [pair] + [at(sign * hop) for hop in (1, 2) for sign in (1, -1)]
    for other in others:
        pl.semaphore_signal(barrier, inc=1, device_id={"gather": other}, device_id_type=MESH)
    window_index = lax.axis_index("tm")
    for step in (1, windows - 1):
        other = lax.rem(window_index + step, windows)
        pl.semaphore_signal(barrier, inc=1, device_id={"tm": other}, device_id_type=MESH)
    for copy in fetches[:3]:
        copy.wait()
    block_ref[...] = ordered(*local[:3])
    mine = [
        pltpu.make_async_copy(held(0, piece), view(0, piece), local_sem.at[piece])
        for piece in range(PIECES)
    ]
    for copy in mine:
        copy.start()
    pl.semaphore_wait(barrier, len(others) + 2)

    def comes(sign, distance, piece):
        return distance < far or (piece < PIECES // 2) == (sign == 1)

    passed, handed = {}, []

    def forward(sign, distance, piece):
        side = 0 if sign == 1 else 1
        for start, stop in HOPS:
            if start == distance and comes(sign, stop, piece):
                passed[sign, stop, piece] = send(
                    -sign * distance,
                    piece,
                    send_sem.at[side, stop - 1, piece],
                    recv_sem.at[side, stop - 1, piece],
                    at(sign * (stop - start)),
                )

    def hand(sign, distance, piece):
        number = distance if sign == 1 or distance in (0, far) else far + distance
        handed.append(
            send(-sign * distance, piece, pair_send.at[number, piece], pair_recv.at[number, piece], pair)
        )

    for piece in range(PIECES):
        forward(1, 0, piece)
        forward(-1, 0, piece)
    for piece in range(PIECES):
        hand(1, 0, piece)
    for copy in fetches[3:]:
        copy.wait()
    for distance in range(1, far + 1):
        for number in range((distance - 1) * len(work) // far, distance * len(work) // far):
            work[number]()
        for piece in range(PIECES):
            for sign in (1, -1):
                if comes(sign, distance, piece):
                    passed[sign, distance, piece].wait_recv()
                    forward(sign, distance, piece)
                    hand(sign, distance, piece)
    for copy in handed:
        copy.wait_recv()
    for copy in mine:
        copy.wait()
    return list(passed.values()) + handed


def compute(
    windows,
    all_ref,
    weight,
    first_ref,
    out_weight_ref,
    bias_ref,
    keep_ref,
    live_ref,
    mask_ref,
    owned_ref,
    index_ref,
    out_ref,
    field,
    first,
    second,
    third,
    send_sem,
    recv_sem,
):
    window_index = lax.axis_index("tm")
    right = lax.rem(window_index + 1, windows)
    left = lax.rem(window_index + windows - 1, windows)
    slots = owned_ref.shape[0]
    comps, span = all_ref.shape[2:]
    tiles = 4

    def turn(group):
        near = [all_ref[index_ref[group * 3 + offset]].reshape(tiles, 32, span) for offset in range(3)]
        for tile in range(tiles):
            stacked = jnp.concatenate([part[tile] for part in near] + [near[0][tile]], axis=0)
            turned = stacked.astype(F32).T
            u = group * tiles + tile
            field[u, pl.ds(HALO, span), :] = jnp.where(
                keep_ref[group] > 0.5, turned, live_ref[u]
            ).astype(BF16)

    copies = []
    for slot in range(slots):
        for group in range(slot * 3, slot * 3 + 3):
            turn(group)
        units = pl.ds(slot * 3 * tiles, 3 * tiles)
        for number, (source, target, device) in enumerate(((span, 0, right), (HALO, HALO + span, left))):
            copy = pltpu.make_async_remote_copy(
                src_ref=field.at[units, pl.ds(source, HALO), :],
                dst_ref=field.at[units, pl.ds(target, HALO), :],
                send_sem=send_sem.at[slot, number],
                recv_sem=recv_sem.at[slot, number],
                device_id={"tm": device},
                device_id_type=MESH,
            )
            copy.start()
            copies.append(copy)

    def ahead(value, by):
        return pltpu.roll(value, value.shape[0] - by, 0)

    def behind(value, by):
        return pltpu.roll(value, by, 0)

    for copy in copies:
        copy.wait()

    before = jnp.where(window_index > 0, 1.0, 0.0).astype(F32)
    after = jnp.where(window_index < windows - 1, 1.0, 0.0).astype(F32)

    def inside(value):
        return jnp.concatenate(
            [value[:HALO] * before, value[HALO : HALO + span], value[HALO + span :] * after], axis=0
        )

    def first_layer(u, carry):
        here = jnp.concatenate(
            [
                (field[u, pl.ds(0, HALO), :].astype(F32) * before).astype(BF16),
                field[u, pl.ds(HALO, span), :],
                (field[u, pl.ds(HALO + span, HALO), :].astype(F32) * after).astype(BF16),
            ],
            axis=0,
        )
        here = jnp.concatenate([here, here], axis=1)
        lifted = [dot(here, first_ref[trace_tap]).astype(BF16) for trace_tap in range(3)]
        sums = [None] * 3
        for trace_tap in range(3):
            for time_tap in range(3):
                term = dot(lifted[trace_tap], weight[21 + trace_tap * 3 + time_tap])
                sums[time_tap] = term if sums[time_tap] is None else sums[time_tap] + term
        total = sums[1] + behind(sums[0], 1) + ahead(sums[2], 1)
        grown = lifted[1].astype(F32) + jnp.maximum(total + bias_ref[0], 0.0)
        first[u] = inside(grown * mask_ref[u]).astype(BF16)
        return carry

    lax.fori_loop(0, slots * 3 * tiles, first_layer, 0, unroll=12)

    def second_layer(v, carry):
        slot, tile = v // tiles, lax.rem(v, tiles)
        sums = [None] * 3
        for trace_tap in range(3):
            u = (slot * 3 + trace_tap) * tiles + tile
            for time_tap in range(3):
                term = dot(first[u], weight[trace_tap * 3 + time_tap])
                sums[time_tap] = term if sums[time_tap] is None else sums[time_tap] + term
        total = sums[1] + behind(sums[0], 4) + ahead(sums[2], 4)
        center = (slot * 3 + 1) * tiles + tile
        grown = first[center].astype(F32) + jnp.maximum(total + bias_ref[1], 0.0)
        second[v] = inside(grown * mask_ref[center]).astype(BF16)
        return carry

    lax.fori_loop(0, slots * tiles, second_layer, 0, unroll=True)

    def third_layer(v, carry):
        slot, tile = v // tiles, lax.rem(v, tiles)
        half = tile // 2
        other = slot * tiles + lax.rem(tile + 2, tiles)
        sums = [
            dot(second[v], weight[9 + time_tap]) + dot(second[other], weight[12 + half * 3 + time_tap])
            for time_tap in range(3)
        ]
        total = sums[1] + behind(sums[0], 2) + ahead(sums[2], 2)
        center = (slot * 3 + 1) * tiles + tile
        grown = second[v].astype(F32) + jnp.maximum(total + bias_ref[2], 0.0)
        third[v] = inside(grown * mask_ref[center]).astype(BF16)
        return carry

    lax.fori_loop(0, slots * tiles, third_layer, 0, unroll=True)

    def fourth_layer(v):
        slot, tile = v // tiles, v % tiles
        early = dot(third[v, pl.ds(0, span + HALO), :], weight[18])[8 : 8 + span]
        middle = dot(third[v, pl.ds(HALO, span), :], weight[19])
        late = dot(third[v, pl.ds(HALO, span + HALO), :], weight[20])[8 : 8 + span]
        center = (slot * 3 + 1) * tiles + tile
        grown = third[v, pl.ds(HALO, span), :].astype(F32) + jnp.maximum(
            early + middle + late + bias_ref[3], 0.0
        )
        grown = (grown * mask_ref[center]).astype(BF16)
        noise = lax.dot_general(
            out_weight_ref[...], grown, (((1,), (1,)), ((), ())), preferred_element_type=F32
        )
        kept = all_ref[index_ref[slot * 9 + 4]].reshape(tiles, 32, span)
        result = (kept[tile].astype(F32) + noise) * owned_ref[slot]
        out_ref[:, tile, slot] = result.reshape(8, comps, span)

    for v in range(slots * tiles):
        fourth_layer(v)


def whole_kernel(holders, windows, *refs):
    sources, out_ref = refs[:9], refs[9]
    local, tables, spread_ref = refs[10:19], refs[19:28], refs[28]
    block_ref, all_ref, layers = refs[29], refs[30], refs[31:35]
    fetch_sem, ring_sems, edge_sems = refs[35], refs[36:41], refs[41:43]
    fetches = []
    for number, (source, target) in enumerate(zip(sources, local)):
        fetches.append(pltpu.make_async_copy(source, target, fetch_sem.at[number]))
        fetches[-1].start()
    work = preparation(*local[:2], *local[3:], *tables, spread_ref)
    sends = share(holders, windows, fetches, work, local, block_ref, all_ref, ring_sems)
    compute(windows, all_ref, *tables, out_ref, *layers, *edge_sems)
    for copy in sends:
        copy.wait_send()


def table_shapes(slots):
    vmem = pltpu.VMEM
    return [
        vmem((30, 256, 256), BF16),
        vmem((3, 256, 256), BF16),
        vmem((32, 256), BF16),
        vmem((4, 1, 256), F32),
        vmem((slots * 3, 1, 128), F32),
        vmem((slots * 12, 1, 128), F32),
        vmem((slots * 12, 1, 256), F32),
        vmem((slots, 1, 128), F32),
        pltpu.SMEM((slots * 12,), jnp.int32),
    ]


def layer_shapes(slots, span):
    rows = span + 2 * HALO
    return [
        pltpu.VMEM((slots * 12, rows, 128), BF16),
        pltpu.VMEM((slots * 12, rows, 256), BF16),
        pltpu.VMEM((slots * 4, rows, 256), BF16),
        pltpu.VMEM((slots * 4, rows, 256), BF16),
    ]


def body(
    records,
    lift_weight,
    lift_bias,
    conv_weight,
    conv_bias,
    out_weight,
    live_count,
    trace_node,
    node_owner,
):
    comps, nodes, span = records.shape[1:]
    holders = lax.axis_size("gather")
    windows = lax.axis_size("tm")
    slots = (nodes + holders - 1) // holders
    far = holders // 4
    sources = (
        live_count,
        trace_node,
        records[0],
        node_owner,
        lift_weight.T,
        lift_bias[None],
        jnp.transpose(conv_weight, (0, 3, 4, 1, 2)),
        conv_bias,
        out_weight,
    )
    local = [
        (pltpu.SMEM if number in (0, 1, 3) else pltpu.VMEM)(source.shape, source.dtype)
        for number, source in enumerate(sources)
    ]
    dma = pltpu.SemaphoreType.DMA
    result = pl.pallas_call(
        functools.partial(whole_kernel, holders, windows),
        out_shape=jax.ShapeDtypeStruct((8, 4, slots, comps, span), F32),
        in_specs=[pl.BlockSpec(memory_space=pltpu.HBM)] * 9,
        out_specs=pl.BlockSpec(memory_space=pltpu.VMEM),
        scratch_shapes=local
        + table_shapes(slots)
        + [
            pltpu.VMEM((36, 32, 256), BF16),
            pltpu.VMEM((nodes, comps, span), BF16),
            pltpu.VMEM((nodes, holders, comps, span), BF16),
        ]
        + layer_shapes(slots, span)
        + [dma((9,)), dma((PIECES,))]
        + [dma((2, far, PIECES))] * 2
        + [dma((2 * far, PIECES))] * 2
        + [dma((slots, 2))] * 2,
        compiler_params=pltpu.CompilerParams(
            collective_id=0, has_side_effects=True, vmem_limit_bytes=60 << 20
        ),
        name="whole",
    )(*sources)
    return jnp.transpose(result, (0, 1, 3, 2, 4)).reshape(32, comps, slots, span)


def solution(mesh):
    return jax.shard_map(
        body,
        mesh=mesh,
        in_specs=(P("gather", None, None, "tm"), P(), P(), P(), P(), P(), P(), P(), P()),
        out_specs=P(None, None, "gather", "tm"),
        check_vma=False,
    )
```
